32 devices in a mesh: rows: 8 (over z, y), var: 4 (over x, core).
Axes of the slice: x: 2, y: 2, z: 4, core: 2. Of those that a mesh axis runs over, the one named last changes fastest.
Arguments:
- signal_matrix: bfloat16 [128, 768, 32], P('rows'), may hold values from -6 to 6
- frame_numbers: int32 [128, 768], P('rows'), may hold values from 0 to 5, as said below
- variate_order: int32 [32], replicated, may hold values from 0 to 31, each once
- embed_weight: bfloat16 [8, 12, 64], P('var'), may hold values from -1.75 to 1.75
- head_weight: bfloat16 [8, 64, 4], P('var'), may hold values from -0.75 to 0.75
- down_a: bfloat16 [6144, 512], replicated, may hold values from -0.078125 to 0.078125
- iso_a: bfloat16 [8192, 512], replicated, may hold values from -0.0625 to 0.0625
- up_a: bfloat16 [512, 6144], replicated, may hold values from -0.25 to 0.25
- down_b: bfloat16 [8192, 512], replicated, may hold values from -0.0625 to 0.0625
- iso_b: bfloat16 [6144, 512], replicated, may hold values from -0.078125 to 0.078125
- up_b: bfloat16 [512, 8192], replicated, may hold values from -0.25 to 0.25
- merge_weight: bfloat16 [1024, 512], replicated, may hold values from -0.1875 to 0.1875
- ff_in: bfloat16 [512, 2048], replicated, may hold values from -0.25 to 0.25
- ff_out: bfloat16 [2048, 512], replicated, may hold values from -0.125 to 0.125
- norm_gains: float32 [3, 512], replicated, may hold values from 0.25 to 1.75
- estimate_cotangent: bfloat16 [128, 768, 32], P('rows', None, 'var'), may hold values from -6 to 6
Outputs:
- prediction: float32 [128, 768, 32], P('rows', None, 'var')
- series_grad: float32 [128, 768, 32], P('rows', None, 'var')
- embed_grad: float32 [8, 12, 64], P('var')
- head_grad: float32 [8, 64, 4], P('var')
- down_a_grad: float32 [6144, 512], P('rows', 'var')
- iso_a_grad: float32 [8192, 512], P('rows', 'var')
- up_a_grad: float32 [512, 6144], P('rows', 'var')
- down_b_grad: float32 [8192, 512], P('rows', 'var')
- iso_b_grad: float32 [6144, 512], P('rows', 'var')
- up_b_grad: float32 [512, 8192], P('rows', 'var')
- merge_grad: float32 [1024, 512], P('rows', 'var')
- ff_in_grad: float32 [512, 2048], P('rows', 'var')
- ff_out_grad: float32 [2048, 512], P('rows', 'var')
- gains_grad: float32 [3, 512], replicated
The draws below stay inside these ranges and needn't reach their ends.
Inputs may be any that keep to these rules, and one draw needn't show every extreme that they name: `frame_numbers`: each row of 768 positions is cut into windows of 96, 144 or 192 positions starting at multiples of 48; the number starts at 0 in each row and rises by one at each window's start; each row's first window has 192 positions. Some row holds six windows. `variate_order`: each variate appears once.
All inputs are finite; a program needn't handle non-finite values.
Results may differ from the reference program's by a relative error of at most 0.019.
Values may be sent and summed in bfloat16 or wider, within the bound.
No kernel may reach another device: no remote copies, remote signals or barrier semaphores. Data moves between devices by JAX's collectives and lax.ppermute only.
A program may use at most 576 MiB of HBM per device.

```python
import jax
import jax.numpy as jnp
import numpy as np
from jax import lax

D = 512
FF = 2048
SA = 12
SB = 16
SLOTS_PER_LINE = 768
CHANNEL_TOTAL = 32
G = 8
ROW_DEV = 4
KA = 16
KB = 12
VPG = 4
DG = 64
EPOCH_LINES = 128


def draw_frame_numbers(key, part):
    layouts = [[4, 4, 4, 4], [4, 2, 4, 3, 3], [4, 3, 3, 2, 4], [4, 4, 2, 2, 4], [4, 3, 2, 3, 4], [4, 2, 2, 2, 2, 4], [4, 2, 3, 4, 3]]
    unit_lookup = np.array([np.repeat(np.arange(len(unit_sizes)), unit_sizes) for unit_sizes in layouts], dtype=np.int32)
    picked_rows = jax.random.randint(key, (EPOCH_LINES,), 0, len(layouts))
    picked_rows = picked_rows.at[0].set(5)
    unit_indices = jnp.asarray(unit_lookup)[picked_rows]
    return jnp.repeat(unit_indices, SLOTS_PER_LINE // unit_lookup.shape[1], axis=1).astype(jnp.int32)


def levels(stream_key, dims, cuts, least, top_value):
    def one(axis_at, shards_of):
        heights = jax.random.uniform(jax.random.fold_in(jax.random.fold_in(stream_key, 6), axis_at), (shards_of,), jnp.float32, least / len(cuts), top_value / len(cuts))
        return jnp.repeat(jnp.exp(heights), dims[axis_at] // shards_of).reshape((-1,) + (1,) * (len(dims) - axis_at - 1))

    level = one(*cuts[0])
    for cut in cuts[1:]:
        level = level * one(*cut)
    return level


def scatter_about(own_key, extent, scale, reach, cuts=(), held_as=jnp.bfloat16):
    drawn = scale * jax.random.normal(own_key, extent, jnp.float32)
    if cuts:
        drawn = drawn * levels(own_key, extent, cuts, -0.22, 0.18)
    return jnp.clip(drawn, -reach, reach).astype(held_as)


def setup_inputs(seed: int = 0) -> dict:
    streams_of = jax.random.split(jax.random.key(seed), 17)
    return {
        "signal_matrix": scatter_about(streams_of[0], (EPOCH_LINES, SLOTS_PER_LINE, CHANNEL_TOTAL), 1.0, 6.0, ((0, 8),)),
        "frame_numbers": draw_frame_numbers(jax.random.fold_in(streams_of[16], 71), 0),
        "variate_order": jax.random.permutation(streams_of[2], CHANNEL_TOTAL).astype(jnp.int32),
        "embed_weight": scatter_about(streams_of[3], (G, 3 * VPG, DG), (3 * VPG) ** -0.5, 1.75, ((0, 4),)),
        "head_weight": scatter_about(streams_of[4], (G, DG, VPG), DG ** -0.5, 0.75, ((0, 4),)),
        "down_a": scatter_about(streams_of[5], (SA * D, D), (SA * D) ** -0.5, 0.078125),
        "iso_a": scatter_about(streams_of[6], (KA * D, D), (KA * D) ** -0.5, 0.0625),
        "up_a": scatter_about(streams_of[7], (D, SA * D), D ** -0.5, 0.25),
        "down_b": scatter_about(streams_of[8], (SB * D, D), (SB * D) ** -0.5, 0.0625),
        "iso_b": scatter_about(streams_of[9], (KB * D, D), (KB * D) ** -0.5, 0.078125),
        "up_b": scatter_about(streams_of[10], (D, SB * D), D ** -0.5, 0.25),
        "merge_weight": scatter_about(streams_of[11], (2 * D, D), (2 * D) ** -0.5, 0.1875),
        "ff_in": scatter_about(streams_of[12], (D, FF), D ** -0.5, 0.25),
        "ff_out": scatter_about(streams_of[13], (FF, D), FF ** -0.5, 0.125),
        "norm_gains": jnp.clip(1.0 + 0.15 * jax.random.normal(streams_of[14], (3, D), jnp.float32), 0.25, 1.75),
        "estimate_cotangent": scatter_about(streams_of[15], (EPOCH_LINES, SLOTS_PER_LINE, CHANNEL_TOTAL), 1.0, 6.0, ((0, 8), (2, 4))),
    }


@jax.custom_vjp
def low(v):
    return lax.optimization_barrier(v.astype(jnp.bfloat16)).astype(jnp.float32)

@jax.custom_vjp
def low_back(v):
    return v

def low_keep(v):
    return (low(v), None)

def low_pass(kept, grad):
    return (grad,)

def back_keep(v):
    return (v, None)

def back_low(kept, grad):
    return (low(grad),)
low.defvjp(low_keep, low_pass)
low_back.defvjp(back_keep, back_low)

def matmul(left, right):
    return jnp.dot(left, right, precision=lax.Precision.HIGHEST, preferred_element_type=jnp.float32)

def shift_rows(values, offset):
    length = values.shape[1]
    if offset == 0:
        return values
    filler = jnp.zeros_like(values[:, :abs(offset)])
    if offset > 0:
        return jnp.concatenate([filler, values[:, :length - offset]], axis=1)
    return jnp.concatenate([values[:, -offset:], filler], axis=1)

def shift_marks(window_marks, offset):
    length = window_marks.shape[1]
    if offset == 0:
        return window_marks
    filler = jnp.full_like(window_marks[:, :abs(offset)], -1)
    if offset > 0:
        return jnp.concatenate([filler, window_marks[:, :length - offset]], axis=1)
    return jnp.concatenate([window_marks[:, -offset:], filler], axis=1)

def same_window(window_marks, offset):
    return (shift_marks(window_marks, offset) == window_marks).astype(jnp.float32)

def window_mean(values, window_marks, half_span):
    running = jnp.zeros_like(values)
    counted = jnp.zeros(window_marks.shape, jnp.float32)
    for offset in range(-half_span, half_span + 1):
        inside = same_window(window_marks, offset)
        running = running + shift_rows(values, offset) * inside[..., None]
        counted = counted + inside
    return running / counted[..., None]

def trend_of(values, window_marks):
    return 0.5 * (window_mean(values, window_marks, 6) + window_mean(values, window_marks, 8))

def layer_norm(values, norm_gain):
    centre = values - lax.optimization_barrier(jnp.mean(values, axis=-1, keepdims=True))
    spread = lax.optimization_barrier(jnp.mean(centre * centre, axis=-1, keepdims=True))
    return centre * lax.rsqrt(spread + 1e-05) * norm_gain

def embed_columns(grouped, window_marks):
    pieces = []
    for offset in (1, 0, -1):
        inside = same_window(window_marks, offset)[:, :, None, None].astype(grouped.dtype)
        pieces.append(shift_rows(grouped, offset) * inside)
    return jnp.concatenate(pieces, axis=-1)

def iso_columns(values, coarse_marks, tap_count):
    pieces = []
    for tap_index in range(tap_count):
        offset = tap_count - 1 - tap_index
        inside = same_window(coarse_marks, offset)[..., None].astype(values.dtype)
        pieces.append(shift_rows(values, offset) * inside)
    return jnp.concatenate(pieces, axis=-1)

def scale_branch(seasonal, seasonal_low, window_marks, down_weight, iso_weight, up_weight, norm_gain, stride):
    row_count, length, feature_count = seasonal.shape
    slot_count = length // stride
    blocks = seasonal_low.reshape(row_count, slot_count, stride * feature_count)
    activated = jnp.tanh(low_back(matmul(blocks, down_weight)))
    columns = iso_columns(low(activated), window_marks[:, ::stride], iso_weight.shape[0] // feature_count)
    second = jnp.tanh(low_back(matmul(columns, iso_weight)))
    joined = layer_norm(second + activated, norm_gain)
    lifted = jnp.tanh(low_back(matmul(low(joined), up_weight)).reshape(row_count, length, feature_count))
    return layer_norm(lifted + seasonal, norm_gain)

def forward(signal_matrix, embed_weight, head_weight, down_a, iso_a, up_a, down_b, iso_b, up_b, merge_weight, ff_in, ff_out, norm_gains, window_marks, variate_order):
    row_count, length, variates = signal_matrix.shape
    groups, tap_width, group_width = embed_weight.shape
    grouped = jnp.take(signal_matrix, variate_order, axis=2).reshape(row_count, length, groups, variates // groups)
    columns = embed_columns(grouped, window_marks)
    embedded = jnp.einsum('rtgk,gkd->rtgd', columns, embed_weight, precision=lax.Precision.HIGHEST)
    hidden = low_back(low(embedded.reshape(row_count, length, groups * group_width)))
    trend_part = trend_of(hidden, window_marks)
    seasonal = hidden - trend_part
    seasonal_low = low(seasonal)
    branch_a = scale_branch(seasonal, seasonal_low, window_marks, down_a, iso_a, up_a, norm_gains[0], SA)
    branch_b = scale_branch(seasonal, seasonal_low, window_marks, down_b, iso_b, up_b, norm_gains[0], SB)
    merged = low_back(matmul(jnp.concatenate([low(branch_a), low(branch_b)], axis=-1), merge_weight))
    mixed = layer_norm(merged, norm_gains[1])
    inner_act = jax.nn.gelu(low_back(matmul(low(mixed), ff_in)), approximate=False)
    outer_act = low_back(matmul(low(inner_act), ff_out))
    result = layer_norm(mixed + outer_act, norm_gains[2]) + trend_part
    result = low_back(low(result)).reshape(row_count, length, groups, group_width)
    predicted = jnp.einsum('rtgd,gdk->rtgk', result, head_weight, precision=lax.Precision.HIGHEST)
    return predicted.reshape(row_count, length, variates)

def reference(signal_matrix, frame_numbers, variate_order, embed_weight, head_weight, down_a, iso_a, up_a, down_b, iso_b, up_b, merge_weight, ff_in, ff_out, norm_gains, estimate_cotangent):
    weights = tuple((weight.astype(jnp.float32) for weight in (embed_weight, head_weight, down_a, iso_a, up_a, down_b, iso_b, up_b, merge_weight, ff_in, ff_out, norm_gains)))
    block_count = EPOCH_LINES // ROW_DEV

    def split_lines(values):
        return values.reshape((block_count, ROW_DEV) + values.shape[1:])

    def step_forward(cumulative_sums, inputs):
        series_block, marks_block, grad_block = inputs

        def local_forward(series_float, *params):
            return forward(series_float, *params, marks_block, variate_order)
        predicted, pullback = jax.vjp(local_forward, series_block.astype(jnp.float32), *weights)
        gradients = pullback(grad_block.astype(jnp.float32))
        grouped_grad = jnp.take(gradients[0], variate_order, axis=2)
        cumulative_sums = tuple((running + gradient for running, gradient in zip(cumulative_sums, gradients[1:])))
        return (cumulative_sums, (predicted, grouped_grad))
    initial_sums = tuple((jnp.zeros_like(weight) for weight in weights))
    cumulative_sums, (predicted_values, signal_adjoint) = lax.scan(step_forward, initial_sums, (split_lines(signal_matrix), split_lines(frame_numbers), split_lines(estimate_cotangent)))
    return (predicted_values.reshape(EPOCH_LINES, SLOTS_PER_LINE, CHANNEL_TOTAL), signal_adjoint.reshape(EPOCH_LINES, SLOTS_PER_LINE, CHANNEL_TOTAL), cumulative_sums[0], cumulative_sums[1], cumulative_sums[2], cumulative_sums[3], cumulative_sums[4], cumulative_sums[5], cumulative_sums[6], cumulative_sums[7], cumulative_sums[8], cumulative_sums[9], cumulative_sums[10], cumulative_sums[11])
```

```python
import jax
import jax.numpy as jnp
from jax import lax
from jax.sharding import PartitionSpec as P

SA = 12
SB = 16


def product(left, right):
    return jnp.dot(left, right, preferred_element_type=jnp.float32)


def shift_rows(values, offset):
    length = values.shape[1]
    if offset == 0:
        return values
    filler = jnp.zeros_like(values[:, : abs(offset)])
    if offset > 0:
        return jnp.concatenate([filler, values[:, : length - offset]], axis=1)
    return jnp.concatenate([values[:, -offset:], filler], axis=1)


def shift_marks(window_marks, offset):
    length = window_marks.shape[1]
    if offset == 0:
        return window_marks
    filler = jnp.full_like(window_marks[:, : abs(offset)], -1)
    if offset > 0:
        return jnp.concatenate([filler, window_marks[:, : length - offset]], axis=1)
    return jnp.concatenate([window_marks[:, -offset:], filler], axis=1)


def same_window(window_marks, offset):
    return (shift_marks(window_marks, offset) == window_marks).astype(jnp.float32)


def window_mean(values, window_marks, half_span):
    running = jnp.zeros_like(values)
    counted = jnp.zeros(window_marks.shape, jnp.float32)
    for offset in range(-half_span, half_span + 1):
        inside = same_window(window_marks, offset)
        running = running + shift_rows(values, offset) * inside[..., None]
        counted = counted + inside
    return running / counted[..., None]


def trend_of(values, window_marks):
    return 0.5 * (window_mean(values, window_marks, 6) + window_mean(values, window_marks, 8))


def layer_norm(values, norm_gain):
    centre = values - jnp.mean(values, axis=-1, keepdims=True)
    spread = jnp.mean(centre * centre, axis=-1, keepdims=True)
    return centre * lax.rsqrt(spread + 1e-05) * norm_gain


def gelu_exact(values):
    return jax.nn.gelu(values, approximate=False)


def embed_columns(grouped, window_marks):
    pieces = []
    for offset in (1, 0, -1):
        inside = same_window(window_marks, offset)[:, :, None, None].astype(grouped.dtype)
        pieces.append(shift_rows(grouped, offset) * inside)
    return jnp.concatenate(pieces, axis=-1)


def iso_columns(values, coarse_marks, tap_count):
    pieces = []
    for tap_index in range(tap_count):
        offset = tap_count - 1 - tap_index
        inside = same_window(coarse_marks, offset)[..., None].astype(values.dtype)
        pieces.append(shift_rows(values, offset) * inside)
    return jnp.concatenate(pieces, axis=-1)


def scale_forward(
    seasonal, seasonal_low, window_marks, down_weight, iso_weight, up_weight, norm_gain, stride
):
    row_count, length, feature_count = seasonal.shape
    slot_count = length // stride
    blocks = seasonal_low.reshape(row_count, slot_count, stride * feature_count)
    activated = jnp.tanh(product(blocks, down_weight))
    coarse_marks = window_marks[:, ::stride]
    tap_count = iso_weight.shape[0] // feature_count
    columns = iso_columns(activated.astype(jnp.bfloat16), coarse_marks, tap_count)
    second = jnp.tanh(product(columns, iso_weight))
    joined_in = second + activated
    joined_low = layer_norm(joined_in, norm_gain).astype(jnp.bfloat16)
    lifted = jnp.tanh(product(joined_low, up_weight)).reshape(row_count, length, feature_count)
    lifted_in = lifted + seasonal
    branch_low = layer_norm(lifted_in, norm_gain).astype(jnp.bfloat16)
    return (
        branch_low,
        (
            blocks,
            activated,
            coarse_marks,
            columns,
            second,
            joined_in,
            joined_low,
            lifted,
            lifted_in,
        ),
    )


def scale_backward(branch_grad, saved, down_weight, iso_weight, up_weight, norm_gain, stride):
    blocks, activated, coarse_marks, columns, second, joined_in, joined_low, lifted, lifted_in = (
        saved
    )
    row_count, length, feature_count = lifted.shape
    slot_count = length // stride
    tap_count = iso_weight.shape[0] // feature_count
    lifted_grad, gain_late = jax.vjp(layer_norm, lifted_in, norm_gain)[1](branch_grad)
    up_pre = (
        (lifted_grad * (1.0 - lifted * lifted))
        .reshape(row_count, slot_count, stride * feature_count)
        .astype(jnp.bfloat16)
    )
    up_grad = jnp.einsum("rnd,rnk->dk", joined_low, up_pre, preferred_element_type=jnp.float32)
    joined_grad = jnp.einsum("rnk,dk->rnd", up_pre, up_weight, preferred_element_type=jnp.float32)
    sum_grad, gain_early = jax.vjp(layer_norm, joined_in, norm_gain)[1](joined_grad)
    iso_pre = (sum_grad * (1.0 - second * second)).astype(jnp.bfloat16)
    iso_grad = jnp.einsum("rnk,rnd->kd", columns, iso_pre, preferred_element_type=jnp.float32)
    column_grad = jnp.einsum("rnd,kd->rnk", iso_pre, iso_weight, preferred_element_type=jnp.float32)
    spread_back = jax.vjp(lambda values: iso_columns(values, coarse_marks, tap_count), activated)[
        1
    ](column_grad)[0]
    act_grad = spread_back + sum_grad
    down_pre = (act_grad * (1.0 - activated * activated)).astype(jnp.bfloat16)
    down_grad = jnp.einsum("rnk,rnd->kd", blocks, down_pre, preferred_element_type=jnp.float32)
    block_grad = jnp.einsum(
        "rnd,kd->rnk", down_pre, down_weight, preferred_element_type=jnp.float32
    )
    seasonal_grad = block_grad.reshape(row_count, length, feature_count) + lifted_grad
    return (seasonal_grad, down_grad, iso_grad, up_grad, gain_early + gain_late)


def mixer_forward(hidden_low, window_marks, mixer_weights, norm_gains):
    down_a, iso_a, up_a, down_b, iso_b, up_b, merge_weight, ff_in, ff_out = mixer_weights
    hidden = hidden_low.astype(jnp.float32)
    trend_part = trend_of(hidden, window_marks)
    seasonal = hidden - trend_part
    seasonal_low = seasonal.astype(jnp.bfloat16)
    branch_a, saved_a = scale_forward(
        seasonal, seasonal_low, window_marks, down_a, iso_a, up_a, norm_gains[0], SA
    )
    branch_b, saved_b = scale_forward(
        seasonal, seasonal_low, window_marks, down_b, iso_b, up_b, norm_gains[0], SB
    )
    stacked = jnp.concatenate([branch_a, branch_b], axis=-1)
    merged = product(stacked, merge_weight)
    mixed = layer_norm(merged, norm_gains[1])
    mixed_low = mixed.astype(jnp.bfloat16)
    inner_pre = product(mixed_low, ff_in)
    inner_low = gelu_exact(inner_pre).astype(jnp.bfloat16)
    outer_act = product(inner_low, ff_out)
    final_in = mixed + outer_act
    result = layer_norm(final_in, norm_gains[2]) + trend_part
    return (
        result,
        (hidden, saved_a, saved_b, stacked, merged, mixed_low, inner_pre, inner_low, final_in),
    )


def mixer_backward(result_grad, saved, window_marks, mixer_weights, norm_gains):
    down_a, iso_a, up_a, down_b, iso_b, up_b, merge_weight, ff_in, ff_out = mixer_weights
    hidden, saved_a, saved_b, stacked, merged, mixed_low, inner_pre, inner_low, final_in = saved
    feature_count = hidden.shape[-1]
    final_grad, gain_last = jax.vjp(layer_norm, final_in, norm_gains[2])[1](result_grad)
    outer_low = final_grad.astype(jnp.bfloat16)
    ff_out_grad = jnp.einsum(
        "rtf,rtd->fd", inner_low, outer_low, preferred_element_type=jnp.float32
    )
    inner_grad = jnp.einsum("rtd,fd->rtf", outer_low, ff_out, preferred_element_type=jnp.float32)
    inner_pre_grad = jax.vjp(gelu_exact, inner_pre)[1](inner_grad)[0].astype(jnp.bfloat16)
    ff_in_grad = jnp.einsum(
        "rtd,rtf->df", mixed_low, inner_pre_grad, preferred_element_type=jnp.float32
    )
    mixed_grad = (
        jnp.einsum("rtf,df->rtd", inner_pre_grad, ff_in, preferred_element_type=jnp.float32)
        + final_grad
    )
    merged_grad, gain_mid = jax.vjp(layer_norm, merged, norm_gains[1])[1](mixed_grad)
    merged_low = merged_grad.astype(jnp.bfloat16)
    merge_grad = jnp.einsum("rtk,rtd->kd", stacked, merged_low, preferred_element_type=jnp.float32)
    stacked_grad = jnp.einsum(
        "rtd,kd->rtk", merged_low, merge_weight, preferred_element_type=jnp.float32
    )
    seasonal_a, down_a_grad, iso_a_grad, up_a_grad, gain_a = scale_backward(
        stacked_grad[..., :feature_count], saved_a, down_a, iso_a, up_a, norm_gains[0], SA
    )
    seasonal_b, down_b_grad, iso_b_grad, up_b_grad, gain_b = scale_backward(
        stacked_grad[..., feature_count:], saved_b, down_b, iso_b, up_b, norm_gains[0], SB
    )
    seasonal_grad = seasonal_a + seasonal_b
    trend_back = jax.vjp(lambda values: trend_of(values, window_marks), hidden)[1](
        result_grad - seasonal_grad
    )[0]
    hidden_grad = seasonal_grad + trend_back
    gains_grad = jnp.stack([gain_a + gain_b, gain_mid, gain_last])
    weight_grads = (
        down_a_grad,
        iso_a_grad,
        up_a_grad,
        down_b_grad,
        iso_b_grad,
        up_b_grad,
        merge_grad,
        ff_in_grad,
        ff_out_grad,
    )
    return (hidden_grad, weight_grads, gains_grad)


def block_diagonal(pieces):
    count, height, width = pieces.shape
    eye = jnp.eye(count, dtype=pieces.dtype)
    spread = pieces[:, :, None, :] * eye[:, None, :, None]
    return spread.reshape(count * height, count * width)


def diagonal_blocks(matrix, count):
    height, width = matrix.shape[0] // count, matrix.shape[1] // count
    blocks = matrix.reshape(count, height, count, width)
    return jnp.stack([blocks[at, :, at, :] for at in range(count)])


def scatter_sum(grad, row_shards, column_shards):
    height, width = grad.shape
    pieces = grad.astype(jnp.bfloat16).reshape(
        row_shards, height // row_shards, column_shards, width // column_shards
    )
    pieces = pieces.transpose(0, 2, 1, 3).reshape(-1, width // column_shards)
    return lax.psum_scatter(pieces, ("rows", "var"), scatter_dimension=0, tiled=True).astype(
        jnp.float32
    )


def body(
    signal_matrix,
    frame_numbers,
    variate_order,
    embed_weight,
    head_weight,
    down_a,
    iso_a,
    up_a,
    down_b,
    iso_b,
    up_b,
    merge_weight,
    ff_in,
    ff_out,
    norm_gains,
    estimate_cotangent,
):
    row_shards, column_shards = lax.axis_size("rows"), lax.axis_size("var")
    var_index = lax.axis_index("var")
    local_rows, length, variates = signal_matrix.shape
    local_groups, tap_width, group_width = embed_weight.shape
    per_group = head_weight.shape[2]
    groups = local_groups * column_shards
    own_variates = variates // column_shards
    time_rows = local_rows // column_shards
    embed_all, head_all = lax.all_gather(
        (embed_weight, head_weight), "var", axis=0, tiled=True
    )
    embed_matrix = jnp.concatenate(
        [
            block_diagonal(embed_all[:, tap * per_group : (tap + 1) * per_group])
            for tap in range(3)
        ],
        axis=0,
    )
    head_matrix = block_diagonal(head_all)
    signal = lax.dynamic_slice_in_dim(signal_matrix, var_index * time_rows, time_rows, 0)
    marks = lax.dynamic_slice_in_dim(frame_numbers, var_index * time_rows, time_rows, 0)
    pick = jax.nn.one_hot(variate_order, variates, dtype=jnp.bfloat16)
    grouped = jnp.einsum("rtv,cv->rtc", signal, pick, preferred_element_type=jnp.float32).astype(
        jnp.bfloat16
    )
    cotangent = lax.all_to_all(
        estimate_cotangent, "var", split_axis=0, concat_axis=2, tiled=True
    )
    embed_cols = embed_columns(grouped[..., None], marks)
    embed_cols = jnp.concatenate([embed_cols[..., tap] for tap in range(3)], axis=-1)
    hidden_low = product(embed_cols, embed_matrix).astype(jnp.bfloat16)
    mixer_weights = (down_a, iso_a, up_a, down_b, iso_b, up_b, merge_weight, ff_in, ff_out)
    result, saved = mixer_forward(hidden_low, marks, mixer_weights, norm_gains)
    result_low = result.astype(jnp.bfloat16)
    predicted = product(result_low, head_matrix)
    head_grad = diagonal_blocks(
        jnp.einsum("rtd,rtk->dk", result_low, cotangent, preferred_element_type=jnp.float32), groups
    )
    result_grad = (
        jnp.einsum("rtk,dk->rtd", cotangent, head_matrix, preferred_element_type=jnp.float32)
        .astype(jnp.bfloat16)
        .astype(jnp.float32)
    )
    hidden_grad, weight_grads, gains_grad = mixer_backward(
        result_grad, saved, marks, mixer_weights, norm_gains
    )
    hidden_grad_low = hidden_grad.astype(jnp.bfloat16)
    embed_full = jnp.einsum(
        "rtk,rtd->kd", embed_cols, hidden_grad_low, preferred_element_type=jnp.float32
    )
    embed_grad = jnp.concatenate(
        [
            diagonal_blocks(embed_full[tap * variates : (tap + 1) * variates], groups)
            for tap in range(3)
        ],
        axis=1,
    )
    column_grad = jnp.einsum(
        "rtd,kd->rtk", hidden_grad_low, embed_matrix, preferred_element_type=jnp.float32
    )
    series_grad = 0.0
    for tap, offset in enumerate((1, 0, -1)):
        inside = same_window(marks, offset)[:, :, None]
        piece = column_grad[..., tap * variates : (tap + 1) * variates] * inside
        series_grad = series_grad + shift_rows(piece, -offset)
    outward = lax.all_to_all(
        jnp.stack([predicted, series_grad]), "var", split_axis=3, concat_axis=1, tiled=True
    )
    embed_sum, head_sum, gains_sum = lax.psum(
        (embed_grad, head_grad, gains_grad), ("rows", "var")
    )
    embed_sum = lax.dynamic_slice_in_dim(embed_sum, var_index * local_groups, local_groups, 0)
    head_sum = lax.dynamic_slice_in_dim(head_sum, var_index * local_groups, local_groups, 0)
    summed = tuple(scatter_sum(grad, row_shards, column_shards) for grad in weight_grads)
    return (outward[0], outward[1], embed_sum, head_sum, *summed, gains_sum)


def solution(mesh):
    placed = (
        P("rows", None, None),
        P("rows", None),
        P(),
        P("var", None, None),
        P("var", None, None),
        P(),
        P(),
        P(),
        P(),
        P(),
        P(),
        P(),
        P(),
        P(),
        P(),
        P("rows", None, "var"),
    )
    return jax.shard_map(
        body,
        mesh=mesh,
        in_specs=placed,
        out_specs=(
            P("rows", None, "var"),
            P("rows", None, "var"),
            P("var", None, None),
            P("var", None, None),
            P("rows", "var"),
            P("rows", "var"),
            P("rows", "var"),
            P("rows", "var"),
            P("rows", "var"),
            P("rows", "var"),
            P("rows", "var"),
            P("rows", "var"),
            P("rows", "var"),
            P(),
        ),
        check_vma=False,
    )
```

```python
import functools

import jax
import jax.numpy as jnp
from jax import lax
from jax.experimental import pallas as pl
from jax.experimental.pallas import tpu as pltpu
from jax.sharding import PartitionSpec as P

SA = 12
SB = 16
F32 = jnp.float32
BF16 = jnp.bfloat16
VMEM_LIMIT = 60 * 1024 * 1024


def nn(left, right):
    return lax.dot_general(left, right, (((1,), (0,)), ((), ())), preferred_element_type=F32)


def nt(left, right):
    return lax.dot_general(left, right, (((1,), (1,)), ((), ())), preferred_element_type=F32)


def tn(left, right):
    return lax.dot_general(left, right, (((0,), (0,)), ((), ())), preferred_element_type=F32)


def flip(values):
    return values.astype(F32).T.astype(BF16)


LANES = 128


def picked(ref, rows):
    return jnp.concatenate([ref[c, rows, :] for c in range(ref.shape[0])], axis=1)


def placed(ref, rows, values):
    for c in range(ref.shape[0]):
        ref[c, rows, :] = values[:, c * LANES : (c + 1) * LANES]


def norm_parts(values):
    centre = values - jnp.mean(values, axis=-1, keepdims=True)
    spread = jnp.mean(centre * centre, axis=-1, keepdims=True)
    scale = lax.rsqrt(spread + 1e-05)
    return centre * scale, scale


def norm_back(grad, unit, scale, gain):
    inner = grad * gain
    first = jnp.mean(inner, axis=-1, keepdims=True)
    second = jnp.mean(inner * unit, axis=-1, keepdims=True)
    return (inner - first - unit * second) * scale, jnp.sum(grad * unit, axis=0, keepdims=True)


def gelu_pair(values):
    size = jnp.abs(values)
    bell = jnp.exp(values * values * -0.5)
    t = 1.0 / (1.0 + size * (0.3275911 * 0.7071067811865476))
    series = t * (
        0.127414796
        + t * (-0.142248368 + t * (0.7107068705 + t * (-0.7265760135 + t * 0.5307027145)))
    )
    tail = series * bell
    below = jnp.where(values >= 0.0, 1.0 - tail, tail)
    return values * below, below + values * bell * 0.3989422804014327


def bands(marks_column, marks_row, row_start, column_start):
    height, width = marks_column.shape[0], marks_row.shape[1]
    here = lax.broadcasted_iota(jnp.int32, (height, width), 0) + row_start
    there = lax.broadcasted_iota(jnp.int32, (height, width), 1) + column_start
    gap = jnp.abs(here - there)
    same = marks_column == marks_row
    near = jnp.where(jnp.logical_and(same, gap <= 6), 1.0, 0.0).astype(BF16)
    wide = jnp.where(jnp.logical_and(same, gap <= 8), 1.0, 0.0).astype(BF16)
    return near, wide


def tiles_of(length):
    tile, span = 256, 512
    return [(at, min(max(at - 128, 0), length - span), tile, span) for at in range(0, length, tile)]


def front_kernel(signal_ref, flags_ref, marks_ref, weight_ref, trend_ref, seasonal_ref, hidden_ref):
    length = signal_ref.shape[0]
    variates = signal_ref.shape[1]
    signal = signal_ref[...].astype(F32)
    before = (pltpu.roll(signal, 1, 0) * flags_ref[:, 0:1]).astype(BF16)
    after = (pltpu.roll(signal, length - 1, 0) * flags_ref[:, 1:2]).astype(BF16)
    hidden = nn(before, weight_ref[0:variates, :])
    hidden = hidden + nn(signal_ref[...], weight_ref[variates : 2 * variates, :])
    hidden = hidden + nn(after, weight_ref[2 * variates : 3 * variates, :])
    hidden_ref[...] = hidden.astype(BF16)
    for at, low, tile, span in tiles_of(length):
        near, wide = bands(
            flags_ref[at : at + tile, 4:5], marks_ref[0, :, low : low + span], at, low
        )
        source = hidden_ref[low : low + span, :]
        trend = nn(near, source) * flags_ref[at : at + tile, 2:3]
        trend = trend + nn(wide, source) * flags_ref[at : at + tile, 3:4]
        trend_ref[at : at + tile, :] = trend
        placed(seasonal_ref, slice(at, at + tile), hidden_ref[at : at + tile, :].astype(F32) - trend)


def front(signal, flags, marks_row, weight, length):
    positions, variates = signal.shape
    width = weight.shape[1]
    whole = lambda shape: pl.BlockSpec(shape, lambda i: (0,) * len(shape))
    return pl.pallas_call(
        front_kernel,
        grid=(positions // length,),
        in_specs=[
            pl.BlockSpec((length, variates), lambda i: (i, 0)),
            pl.BlockSpec((length, flags.shape[1]), lambda i: (i, 0)),
            pl.BlockSpec((1, 1, length), lambda i: (i, 0, 0)),
            whole(weight.shape),
        ],
        out_specs=[
            pl.BlockSpec((length, width), lambda i: (i, 0)),
            pl.BlockSpec((width // LANES, length, LANES), lambda i: (0, i, 0)),
        ],
        out_shape=[
            jax.ShapeDtypeStruct((positions, width), F32),
            jax.ShapeDtypeStruct((width // LANES, positions, LANES), F32),
        ],
        scratch_shapes=[pltpu.VMEM((length, width), BF16)],
        compiler_params=pltpu.CompilerParams(vmem_limit_bytes=VMEM_LIMIT),
        name="front",
    )(signal, flags, marks_row, weight)


def scale_forward_kernel(
    stride, taps, step_taps,
    seasonal_ref, down_ref, iso_ref, up_ref, since_ref, gain_ref,
    lifted_ref, act_ref, second_ref, joined_ref,
    total,
):
    step = pl.program_id(0)
    blocks, width = act_ref.shape
    down_steps, iso_steps = stride // step_taps, taps // step_taps

    @pl.when(step == 0)
    def _():
        total[...] = jnp.zeros_like(total)

    @pl.when(step < down_steps)
    def _():
        sums = total[...]
        for k in range(step_taps):
            rows = picked(seasonal_ref, pl.ds(step * step_taps + k, blocks, stride=stride))
            sums = sums + nn(rows.astype(BF16), down_ref[k * width : (k + 1) * width, :])
        total[...] = sums

    @pl.when(step == down_steps - 1)
    def _():
        active = jnp.tanh(total[...])
        act_ref[...] = active
        total[...] = jnp.zeros_like(total)

    @pl.when(jnp.logical_and(step >= down_steps, step < down_steps + iso_steps))
    def _():
        sums = total[...]
        for k in range(step_taps):
            back = taps - 1 - ((step - down_steps) * step_taps + k)
            rows = pltpu.roll(act_ref[...], back, 0)
            rows = jnp.where(since_ref[...] >= back, rows, 0.0).astype(BF16)
            sums = sums + nn(rows, iso_ref[k * width : (k + 1) * width, :])
        total[...] = sums

    @pl.when(step == down_steps + iso_steps - 1)
    def _():
        second = jnp.tanh(total[...])
        second_ref[...] = second
        unit, _ = norm_parts(second + act_ref[...])
        joined_ref[...] = (unit * gain_ref[0:1, :]).astype(BF16)

    @pl.when(step >= down_steps + iso_steps)
    def _():
        for k in range(step_taps):
            lifted = nn(joined_ref[...], up_ref[:, k * width : (k + 1) * width])
            lifted_ref[k] = jnp.tanh(lifted).astype(BF16)


def scale_forward(seasonal, down, iso, up, since, gains, stride):
    width, positions = down.shape[1], seasonal.shape[1]
    blocks = positions // stride
    taps = iso.shape[0] // width
    step_taps = 2
    ds, isteps = stride // step_taps, taps // step_taps
    whole = lambda shape: pl.BlockSpec(
        shape, lambda t: (0,) * len(shape), pipeline_mode=pl.Buffered(1)
    )
    clip = lambda value, top: jnp.minimum(jnp.maximum(value, 0), top)
    return pl.pallas_call(
        functools.partial(scale_forward_kernel, stride, taps, step_taps),
        grid=(2 * ds + isteps,),
        in_specs=[
            whole(seasonal.shape),
            pl.BlockSpec((step_taps * width, width), lambda t: (clip(t, ds - 1), 0)),
            pl.BlockSpec((step_taps * width, width), lambda t: (clip(t - ds, isteps - 1), 0)),
            pl.BlockSpec((width, step_taps * width), lambda t: (0, clip(t - ds - isteps, ds - 1))),
            whole(since.shape),
            whole(gains.shape),
        ],
        out_specs=[
            pl.BlockSpec(
                (step_taps, blocks, width), lambda t: (clip(t - ds - isteps, ds - 1), 0, 0)
            ),
            pl.BlockSpec((blocks, width), lambda t: (0, 0)),
            pl.BlockSpec((blocks, width), lambda t: (0, 0)),
            pl.BlockSpec((blocks, width), lambda t: (0, 0)),
        ],
        out_shape=[
            jax.ShapeDtypeStruct((stride, blocks, width), BF16),
            jax.ShapeDtypeStruct((blocks, width), F32),
            jax.ShapeDtypeStruct((blocks, width), F32),
            jax.ShapeDtypeStruct((blocks, width), BF16),
        ],
        scratch_shapes=[pltpu.VMEM((blocks, width), F32)],
        compiler_params=pltpu.CompilerParams(vmem_limit_bytes=VMEM_LIMIT),
        name="scale_forward",
    )(seasonal, down, iso, up, since, gains)


def tail_kernel(
    lifted_a_ref, lifted_b_ref, seasonal_ref, trend_ref, cot_ref,
    merge_ref, ff_in_ref, ff_out_ref, head_ref, gains_ref,
    pred_ref, up_a_ref, up_b_ref, sres_ref,
    merge_out, ff_in_out, ff_out_out, head_out, gains_out,
    wide_a, wide_b, inner_all, pre_all, slope, mixed_all, outer_all, merged_all, stacked_all,
    result_all, merge_sum, ff_in_sum, ff_out_sum,
):
    row = pl.program_id(0)
    length, width = trend_ref.shape
    hidden = ff_in_ref.shape[1]
    tile, chunk = 256, 512
    stride_a, per_a = lifted_a_ref.shape[0], lifted_a_ref.shape[1]
    stride_b, per_b = lifted_b_ref.shape[0], lifted_b_ref.shape[1]

    @pl.when(row == 0)
    def _():
        merge_sum[...] = jnp.zeros_like(merge_sum)
        ff_in_sum[...] = jnp.zeros_like(ff_in_sum)
        ff_out_sum[...] = jnp.zeros_like(ff_out_sum)
        head_out[...] = jnp.zeros_like(head_out)
        gains_out[...] = jnp.zeros_like(gains_out)

    for j in range(stride_a):
        placed(wide_a, pl.ds(j, per_a, stride=stride_a), lifted_a_ref[j].astype(F32))
    for j in range(stride_b):
        placed(wide_b, pl.ds(j, per_b, stride=stride_b), lifted_b_ref[j].astype(F32))
    gain_0, gain_1, gain_2 = gains_ref[0:1, :], gains_ref[1:2, :], gains_ref[2:3, :]

    def part(at, carry):
        rows = pl.ds(pl.multiple_of(at * tile, tile), tile)
        seasonal = picked(seasonal_ref, rows)
        unit_a, scale_a = norm_parts(picked(wide_a, rows) + seasonal)
        unit_b, scale_b = norm_parts(picked(wide_b, rows) + seasonal)
        branch_a = (unit_a * gain_0).astype(BF16)
        branch_b = (unit_b * gain_0).astype(BF16)
        stacked_all[rows, 0:width] = branch_a
        stacked_all[rows, width : 2 * width] = branch_b
        merged = nn(branch_a, merge_ref[0:width, :]) + nn(branch_b, merge_ref[width:, :])
        unit_1, scale_1 = norm_parts(merged)
        mixed = unit_1 * gain_1
        mixed_low = mixed.astype(BF16)
        mixed_all[rows, :] = mixed_low
        total = mixed
        for c in range(0, hidden, chunk):
            inner, fall = gelu_pair(nn(mixed_low, ff_in_ref[:, c : c + chunk]))
            inner_low = inner.astype(BF16)
            inner_all[rows, c : c + chunk] = inner_low
            slope[:, c : c + chunk] = fall.astype(BF16)
            total = total + nn(inner_low, ff_out_ref[c : c + chunk, :])
        unit_2, scale_2 = norm_parts(total)
        result_low = (unit_2 * gain_2 + trend_ref[rows, :]).astype(BF16)
        result_all[rows, :] = result_low
        pred_ref[rows, :] = nn(result_low, head_ref[...])
        result_grad = nt(cot_ref[rows, :], head_ref[...]).astype(BF16).astype(F32)
        final_grad, gain_grad_2 = norm_back(result_grad, unit_2, scale_2, gain_2)
        outer_low = final_grad.astype(BF16)
        outer_all[rows, :] = outer_low
        mixed_grad = final_grad
        for c in range(0, hidden, chunk):
            back = nt(outer_low, ff_out_ref[c : c + chunk, :])
            pre_low = (back * slope[:, c : c + chunk].astype(F32)).astype(BF16)
            pre_all[rows, c : c + chunk] = pre_low
            mixed_grad = mixed_grad + nt(pre_low, ff_in_ref[:, c : c + chunk])
        merged_grad, gain_grad_1 = norm_back(mixed_grad, unit_1, scale_1, gain_1)
        merged_low = merged_grad.astype(BF16)
        merged_all[rows, :] = merged_low
        lifted_a_grad, gain_grad_a = norm_back(
            nt(merged_low, merge_ref[0:width, :]), unit_a, scale_a, gain_0
        )
        lifted_b_grad, gain_grad_b = norm_back(
            nt(merged_low, merge_ref[width:, :]), unit_b, scale_b, gain_0
        )
        sres_ref[rows, :] = lifted_a_grad + lifted_b_grad
        value = picked(wide_a, rows)
        placed(wide_a, rows, lifted_a_grad * (1.0 - value * value))
        value = picked(wide_b, rows)
        placed(wide_b, rows, lifted_b_grad * (1.0 - value * value))
        gains_out[0:1, :] += gain_grad_a + gain_grad_b
        gains_out[1:2, :] += gain_grad_1
        gains_out[2:3, :] += gain_grad_2
        return carry

    lax.fori_loop(0, length // tile, part, 0)
    for j in range(stride_a):
        up_a_ref[j] = picked(wide_a, pl.ds(j, per_a, stride=stride_a)).astype(BF16)
    for j in range(stride_b):
        up_b_ref[j] = picked(wide_b, pl.ds(j, per_b, stride=stride_b)).astype(BF16)
    mixed_t, outer_t, merged_t = flip(mixed_all[...]), flip(outer_all[...]), flip(merged_all[...])
    for c in range(0, hidden, chunk):
        ff_in_sum[:, c : c + chunk] += nn(mixed_t, pre_all[:, c : c + chunk])
        ff_out_sum[:, c : c + chunk] += nn(outer_t, inner_all[:, c : c + chunk])
    for c in range(0, 2 * width, chunk):
        merge_sum[:, c : c + chunk] += nn(merged_t, stacked_all[:, c : c + chunk])
    head_out[...] += tn(result_all[...], cot_ref[...])

    @pl.when(row == pl.num_programs(0) - 1)
    def _():
        for k in range(merge_out.shape[0]):
            size = merge_out.shape[2]
            merge_out[k] = merge_sum[:, k * size : (k + 1) * size].astype(BF16)
        for k in range(ff_in_out.shape[0]):
            size = ff_in_out.shape[2]
            ff_in_out[k] = ff_in_sum[:, k * size : (k + 1) * size].astype(BF16)
        for k in range(ff_out_out.shape[0]):
            size = ff_out_out.shape[2]
            ff_out_out[k] = ff_out_sum[:, k * size : (k + 1) * size].astype(BF16)


def tail(lifted_a, lifted_b, seasonal, trend, cot, merge, ff_in, ff_out, head, gains, length):
    positions, width = trend.shape
    hidden = ff_in.shape[1]
    outs = cot.shape[1]
    stride_a, stride_b = lifted_a.shape[0], lifted_b.shape[0]
    per_a, per_b = length // stride_a, length // stride_b
    fixed = lambda shape: pl.BlockSpec(
        shape, lambda i: (0,) * len(shape), pipeline_mode=pl.Buffered(1)
    )
    kept = lambda shape: pl.BlockSpec(shape, lambda i: (0,) * len(shape))
    by_row = lambda size: pl.BlockSpec((length, size), lambda i: (i, 0))
    by_tap = lambda taps, per: pl.BlockSpec((taps, per, width), lambda i: (0, i, 0))
    pieces = ((8, width, 128), (4, width, 512), (8, width, 256))
    return pl.pallas_call(
        tail_kernel,
        grid=(positions // length,),
        in_specs=[
            by_tap(stride_a, per_a), by_tap(stride_b, per_b),
            pl.BlockSpec((width // LANES, length, LANES), lambda i: (0, i, 0)), by_row(width),
            by_row(outs), fixed(merge.shape), fixed(ff_in.shape), fixed(ff_out.shape),
            fixed(head.shape), fixed(gains.shape),
        ],
        out_specs=[
            by_row(outs), by_tap(stride_a, per_a), by_tap(stride_b, per_b), by_row(width),
            *[fixed(piece) for piece in pieces], kept((width, outs)), kept(gains.shape),
        ],
        out_shape=[
            jax.ShapeDtypeStruct((positions, outs), F32),
            jax.ShapeDtypeStruct(lifted_a.shape, BF16),
            jax.ShapeDtypeStruct(lifted_b.shape, BF16),
            jax.ShapeDtypeStruct((positions, width), F32),
            *[jax.ShapeDtypeStruct(piece, BF16) for piece in pieces],
            jax.ShapeDtypeStruct((width, outs), F32),
            jax.ShapeDtypeStruct(gains.shape, F32),
        ],
        scratch_shapes=[
            pltpu.VMEM((width // LANES, length, LANES), F32),
            pltpu.VMEM((width // LANES, length, LANES), F32),
            pltpu.VMEM((length, hidden), BF16), pltpu.VMEM((length, hidden), BF16),
            pltpu.VMEM((256, hidden), BF16), pltpu.VMEM((length, width), BF16),
            pltpu.VMEM((length, width), BF16), pltpu.VMEM((length, width), BF16),
            pltpu.VMEM((length, 2 * width), BF16), pltpu.VMEM((length, width), BF16),
            pltpu.VMEM((width, 2 * width), F32), pltpu.VMEM((width, hidden), F32),
            pltpu.VMEM((width, hidden), F32),
        ],
        compiler_params=pltpu.CompilerParams(vmem_limit_bytes=VMEM_LIMIT),
        name="tail",
    )(lifted_a, lifted_b, seasonal, trend, cot, merge, ff_in, ff_out, head, gains)


def scale_backward_kernel(
    stride, taps, step_taps,
    pre_ref, up_ref, iso_ref, down_ref, act_ref, second_ref, since_ref, gain_ref,
    iso_pre_ref, down_pre_ref, block_ref, gain_out,
    total, spread,
):
    step = pl.program_id(0)
    blocks, width = act_ref.shape
    up_steps, iso_steps = stride // step_taps, taps // step_taps

    @pl.when(step == 0)
    def _():
        total[...] = jnp.zeros_like(total)
        spread[...] = jnp.zeros_like(spread)

    @pl.when(step < up_steps)
    def _():
        sums = total[...]
        for k in range(step_taps):
            sums = sums + nt(pre_ref[k], up_ref[:, k * width : (k + 1) * width])
        total[...] = sums

    @pl.when(step == up_steps - 1)
    def _():
        second = second_ref[...]
        unit, scale = norm_parts(second + act_ref[...])
        sum_grad, gain_grad = norm_back(total[...], unit, scale, gain_ref[0:1, :])
        gain_out[...] = gain_grad
        iso_pre_ref[...] = (sum_grad * (1.0 - second * second)).astype(BF16)
        spread[...] = sum_grad

    @pl.when(jnp.logical_and(step >= up_steps, step < up_steps + iso_steps))
    def _():
        for k in range(step_taps):
            back = taps - 1 - ((step - up_steps) * step_taps + k)
            grad = nt(iso_pre_ref[...], iso_ref[k * width : (k + 1) * width, :])
            grad = jnp.where(since_ref[...] >= back, grad, 0.0)
            spread[...] += pltpu.roll(grad, blocks - back, 0)

    @pl.when(step == up_steps + iso_steps - 1)
    def _():
        active = act_ref[...]
        down_pre_ref[...] = (spread[...] * (1.0 - active * active)).astype(BF16)

    @pl.when(step >= up_steps + iso_steps)
    def _():
        for k in range(step_taps):
            block_ref[k] = nt(
                down_pre_ref[...], down_ref[k * width : (k + 1) * width, :]
            ).astype(BF16)


def scale_backward(pre, up, iso, down, act, second, since, gains):
    stride, blocks, width = pre.shape
    taps = iso.shape[0] // width
    step_taps = 2
    us, isteps = stride // step_taps, taps // step_taps
    whole = lambda shape: pl.BlockSpec(
        shape, lambda t: (0,) * len(shape), pipeline_mode=pl.Buffered(1)
    )
    clip = lambda value, top: jnp.minimum(jnp.maximum(value, 0), top)
    return pl.pallas_call(
        functools.partial(scale_backward_kernel, stride, taps, step_taps),
        grid=(2 * us + isteps,),
        in_specs=[
            pl.BlockSpec((step_taps, blocks, width), lambda t: (clip(t, us - 1), 0, 0)),
            pl.BlockSpec((width, step_taps * width), lambda t: (0, clip(t, us - 1))),
            pl.BlockSpec((step_taps * width, width), lambda t: (clip(t - us, isteps - 1), 0)),
            pl.BlockSpec(
                (step_taps * width, width), lambda t: (clip(t - us - isteps, us - 1), 0)
            ),
            whole(act.shape), whole(second.shape), whole(since.shape), whole(gains.shape),
        ],
        out_specs=[
            pl.BlockSpec((blocks, width), lambda t: (0, 0)),
            pl.BlockSpec((blocks, width), lambda t: (0, 0)),
            pl.BlockSpec(
                (step_taps, blocks, width), lambda t: (clip(t - us - isteps, us - 1), 0, 0)
            ),
            pl.BlockSpec((1, width), lambda t: (0, 0)),
        ],
        out_shape=[
            jax.ShapeDtypeStruct((blocks, width), BF16),
            jax.ShapeDtypeStruct((blocks, width), BF16),
            jax.ShapeDtypeStruct((stride, blocks, width), BF16),
            jax.ShapeDtypeStruct((1, width), F32),
        ],
        scratch_shapes=[pltpu.VMEM((blocks, width), F32), pltpu.VMEM((blocks, width), F32)],
        compiler_params=pltpu.CompilerParams(vmem_limit_bytes=VMEM_LIMIT),
        name="scale_backward",
    )(pre, up, iso, down, act, second, since, gains)


def up_grad_kernel(joined_ref, pre_ref, out_ref, turned):
    @pl.when(pl.program_id(0) == 0)
    def _():
        turned[...] = flip(joined_ref[...])

    for k in range(pre_ref.shape[0]):
        out_ref[k] = nn(turned[...], pre_ref[k]).astype(BF16)


def up_grad(joined, pre):
    stride, blocks, width = pre.shape
    step_taps = 2
    return pl.pallas_call(
        up_grad_kernel,
        grid=(stride // step_taps,),
        in_specs=[
            pl.BlockSpec((blocks, width), lambda t: (0, 0)),
            pl.BlockSpec((step_taps, blocks, width), lambda t: (t, 0, 0)),
        ],
        out_specs=pl.BlockSpec((step_taps, width, width), lambda t: (t, 0, 0)),
        out_shape=jax.ShapeDtypeStruct((stride, width, width), BF16),
        scratch_shapes=[pltpu.VMEM((width, blocks), BF16)],
        compiler_params=pltpu.CompilerParams(vmem_limit_bytes=VMEM_LIMIT),
        name="up_grad",
    )(joined, pre)


def store_halves(out_ref, k, product):
    half = out_ref.shape[2]
    out_ref[2 * k] = product[:, :half].astype(BF16)
    out_ref[2 * k + 1] = product[:, half:].astype(BF16)


def iso_grad_kernel(taps, step_taps, pre_ref, act_ref, since_ref, out_ref, turned):
    step = pl.program_id(0)
    blocks, width = act_ref.shape

    @pl.when(step == 0)
    def _():
        turned[...] = flip(pre_ref[...])

    for k in range(step_taps):
        back = taps - 1 - (step * step_taps + k)
        rows = pltpu.roll(act_ref[...], back, 0)
        rows = jnp.where(since_ref[...] >= back, rows, 0.0).astype(BF16)
        store_halves(out_ref, k, nn(turned[...], rows))


def iso_grad(pre, act, since, taps):
    blocks, width = act.shape
    step_taps = 2
    whole = lambda shape: pl.BlockSpec(shape, lambda t: (0,) * len(shape))
    return pl.pallas_call(
        functools.partial(iso_grad_kernel, taps, step_taps),
        grid=(taps // step_taps,),
        in_specs=[whole(pre.shape), whole(act.shape), whole(since.shape)],
        out_specs=pl.BlockSpec((2 * step_taps, width, width // 2), lambda t: (t, 0, 0)),
        out_shape=jax.ShapeDtypeStruct((2 * taps, width, width // 2), BF16),
        scratch_shapes=[pltpu.VMEM((width, blocks), BF16)],
        compiler_params=pltpu.CompilerParams(vmem_limit_bytes=VMEM_LIMIT),
        name="iso_grad",
    )(pre, act, since)


def down_grad_kernel(stride, step_taps, pre_ref, seasonal_ref, out_ref, turned):
    step = pl.program_id(0)
    blocks = pre_ref.shape[0]

    @pl.when(step == 0)
    def _():
        turned[...] = flip(pre_ref[...])

    for k in range(step_taps):
        rows = picked(seasonal_ref, pl.ds(step * step_taps + k, blocks, stride=stride))
        store_halves(out_ref, k, nn(turned[...], rows.astype(BF16)))


def down_grad(pre, seasonal):
    blocks, width = pre.shape
    stride = seasonal.shape[1] // blocks
    step_taps = 2
    whole = lambda shape: pl.BlockSpec(
        shape, lambda t: (0,) * len(shape), pipeline_mode=pl.Buffered(1)
    )
    return pl.pallas_call(
        functools.partial(down_grad_kernel, stride, step_taps),
        grid=(stride // step_taps,),
        in_specs=[whole(pre.shape), whole(seasonal.shape)],
        out_specs=pl.BlockSpec((2 * step_taps, width, width // 2), lambda t: (t, 0, 0)),
        out_shape=jax.ShapeDtypeStruct((2 * stride, width, width // 2), BF16),
        scratch_shapes=[pltpu.VMEM((width, blocks), BF16)],
        compiler_params=pltpu.CompilerParams(vmem_limit_bytes=VMEM_LIMIT),
        name="down_grad",
    )(pre, seasonal)


def back_kernel(
    sres_ref, block_a_ref, block_b_ref, cot_ref, head_ref, signal_ref, flags_ref, marks_ref,
    weight_ref, series_ref, embed_ref, season, low_near, low_wide, hidden,
):
    length, width = sres_ref.shape
    variates = signal_ref.shape[1]
    stride_a, per_a = block_a_ref.shape[0], block_a_ref.shape[1]
    stride_b, per_b = block_b_ref.shape[0], block_b_ref.shape[1]

    @pl.when(pl.program_id(0) == 0)
    def _():
        embed_ref[...] = jnp.zeros_like(embed_ref)

    placed(season, slice(0, length), sres_ref[...])
    for j in range(stride_a):
        at = pl.ds(j, per_a, stride=stride_a)
        placed(season, at, picked(season, at) + block_a_ref[j].astype(F32))
    for j in range(stride_b):
        at = pl.ds(j, per_b, stride=stride_b)
        placed(season, at, picked(season, at) + block_b_ref[j].astype(F32))
    result_grad = nt(cot_ref[...], head_ref[...]).astype(BF16).astype(F32)
    gap = result_grad - picked(season, slice(0, length))
    low_near[...] = (gap * flags_ref[:, 2:3]).astype(BF16)
    low_wide[...] = (gap * flags_ref[:, 3:4]).astype(BF16)
    for at, low, tile, span in tiles_of(length):
        near, wide = bands(
            flags_ref[at : at + tile, 4:5], marks_ref[0, :, low : low + span], at, low
        )
        total = picked(season, slice(at, at + tile)) + nn(near, low_near[low : low + span, :])
        total = total + nn(wide, low_wide[low : low + span, :])
        hidden[at : at + tile, :] = total.astype(BF16)
    grad = hidden[...]
    first = nt(grad, weight_ref[0:variates, :]) * flags_ref[:, 0:1]
    last = nt(grad, weight_ref[2 * variates :, :]) * flags_ref[:, 1:2]
    series_ref[...] = (
        nt(grad, weight_ref[variates : 2 * variates, :])
        + pltpu.roll(first, length - 1, 0)
        + pltpu.roll(last, 1, 0)
    )
    signal = signal_ref[...].astype(F32)
    before = (pltpu.roll(signal, 1, 0) * flags_ref[:, 0:1]).astype(BF16)
    after = (pltpu.roll(signal, length - 1, 0) * flags_ref[:, 1:2]).astype(BF16)
    embed_ref[0:variates, :] += tn(before, grad)
    embed_ref[variates : 2 * variates, :] += tn(signal_ref[...], grad)
    embed_ref[2 * variates :, :] += tn(after, grad)


def back(sres, block_a, block_b, cot, head, signal, flags, marks_row, weight, length):
    positions, width = sres.shape
    variates = signal.shape[1]
    stride_a, stride_b = block_a.shape[0], block_b.shape[0]
    whole = lambda shape: pl.BlockSpec(shape, lambda i: (0,) * len(shape))
    by_row = lambda size: pl.BlockSpec((length, size), lambda i: (i, 0))
    return pl.pallas_call(
        back_kernel,
        grid=(positions // length,),
        in_specs=[
            by_row(width),
            pl.BlockSpec((stride_a, length // stride_a, width), lambda i: (0, i, 0)),
            pl.BlockSpec((stride_b, length // stride_b, width), lambda i: (0, i, 0)),
            by_row(cot.shape[1]), whole(head.shape), by_row(variates), by_row(flags.shape[1]),
            pl.BlockSpec((1, 1, length), lambda i: (i, 0, 0)), whole(weight.shape),
        ],
        out_specs=[by_row(variates), whole(weight.shape)],
        out_shape=[
            jax.ShapeDtypeStruct((positions, variates), F32),
            jax.ShapeDtypeStruct(weight.shape, F32),
        ],
        scratch_shapes=[
            pltpu.VMEM((width // LANES, length, LANES), F32), pltpu.VMEM((length, width), BF16),
            pltpu.VMEM((length, width), BF16), pltpu.VMEM((length, width), BF16),
        ],
        compiler_params=pltpu.CompilerParams(vmem_limit_bytes=VMEM_LIMIT),
        name="back",
    )(sres, block_a, block_b, cot, head, signal, flags, marks_row, weight)


def block_diagonal(pieces):
    count, height, width = pieces.shape
    eye = jnp.eye(count, dtype=pieces.dtype)
    spread = pieces[:, :, None, :] * eye[:, None, :, None]
    return spread.reshape(count * height, count * width)


def diagonal_blocks(matrix, count):
    height, width = matrix.shape[0] // count, matrix.shape[1] // count
    blocks = matrix.reshape(count, height, count, width)
    return jnp.stack([blocks[at, :, at, :] for at in range(count)])


def same_window(marks, offset):
    length = marks.shape[1]
    filler = jnp.full_like(marks[:, : abs(offset)], -1)
    if offset > 0:
        moved = jnp.concatenate([filler, marks[:, : length - offset]], axis=1)
    else:
        moved = jnp.concatenate([marks[:, -offset:], filler], axis=1)
    return (moved == marks).astype(F32)


def window_flags(marks):
    near = jnp.ones(marks.shape, F32)
    for offset in range(1, 7):
        near = near + same_window(marks, offset) + same_window(marks, -offset)
    wide = near
    for offset in range(7, 9):
        wide = wide + same_window(marks, offset) + same_window(marks, -offset)
    zero = jnp.zeros_like(near)
    columns = [
        same_window(marks, 1), same_window(marks, -1), 0.5 / near, 0.5 / wide,
        marks.astype(F32), zero, zero, zero,
    ]
    return jnp.stack(columns, axis=-1).reshape(-1, len(columns))


def blocks_since_start(marks, stride, taps):
    coarse = marks[:, ::stride]
    since = jnp.zeros(coarse.shape, F32)
    for offset in range(1, taps):
        since = since + same_window(coarse, offset)
    return since.astype(jnp.int32).reshape(-1, 1)


def log2_of(size):
    return size.bit_length() - 1


def exchange(parts, axis, bit_axis, bit):
    rows, columns = lax.axis_size("rows"), lax.axis_size("var")
    mine = (lax.axis_index(bit_axis) >> bit) & 1
    pairs = []
    for r in range(rows):
        for c in range(columns):
            to = (r ^ (1 << bit), c) if bit_axis == "rows" else (r, c ^ (1 << bit))
            pairs.append((r * columns + c, to[0] * columns + to[1]))
    sent = lax.dynamic_index_in_dim(parts, 1 - mine, axis, keepdims=False)
    kept = lax.dynamic_index_in_dim(parts, mine, axis, keepdims=False)
    got = lax.ppermute(sent, ("rows", "var"), pairs)
    return (kept.astype(F32) + got.astype(F32)).astype(BF16)


def scatter_sum(grad, by_rows, order, shape):
    rows, columns = lax.axis_size("rows"), lax.axis_size("var")
    count, width, size = grad.shape
    outer, inner = (rows, columns) if by_rows else (columns, rows)
    names = ("rows", "var") if by_rows else ("var", "rows")
    if count % outer or width % (16 * inner) or rows & (rows - 1) or columns & (columns - 1):
        full = grad.transpose(1, 0, 2).reshape(width, count * size)
        full = full.T if by_rows else full
        height, depth = full.shape
        full = full.reshape(rows, height // rows, columns, depth // columns)
        full = full.transpose(0, 2, 1, 3).reshape(-1, depth // columns)
        return lax.psum_scatter(full, ("rows", "var"), scatter_dimension=0, tiled=True).astype(F32)
    labels = [(names[0], bit) for bit in reversed(range(log2_of(outer)))]
    labels += [None]
    labels += [(names[1], bit) for bit in reversed(range(log2_of(inner)))]
    parts = grad.reshape(
        (2,) * log2_of(outer) + (count // outer,) + (2,) * log2_of(inner) + (width // inner, size)
    )
    for label in order(log2_of(rows), log2_of(columns)):
        axis = labels.index(label)
        parts = exchange(parts, axis, *label)
        labels.pop(axis)
    parts = parts.astype(F32)
    if by_rows:
        return parts.transpose(0, 2, 1).reshape(shape)
    return parts.transpose(1, 0, 2).reshape(shape)


def across_first(row_bits, column_bits):
    return [("var", bit) for bit in range(column_bits)] + [("rows", bit) for bit in range(row_bits)]


def rows_first(row_bits, column_bits):
    return (
        [("var", 0), ("rows", 0)]
        + [("var", bit) for bit in range(1, column_bits)]
        + [("rows", bit) for bit in range(1, row_bits)]
    )


def body(
    signal_matrix, frame_numbers, variate_order, embed_weight, head_weight,
    down_a, iso_a, up_a, down_b, iso_b, up_b, merge_weight, ff_in, ff_out,
    norm_gains, estimate_cotangent,
):
    rows, columns = lax.axis_size("rows"), lax.axis_size("var")
    var_index = lax.axis_index("var")
    local_rows, length, variates = signal_matrix.shape
    local_groups = embed_weight.shape[0]
    per_group = head_weight.shape[2]
    groups = local_groups * columns
    time_rows = local_rows // columns
    width = norm_gains.shape[1]
    embed_all, head_all = lax.all_gather((embed_weight, head_weight), "var", axis=0, tiled=True)
    cotangent = lax.all_to_all(
        estimate_cotangent, "var", split_axis=0, concat_axis=2, tiled=True
    ).reshape(-1, variates)
    pick = jax.nn.one_hot(variate_order, variates, dtype=BF16)
    by_group = [
        block_diagonal(embed_all[:, tap * per_group : (tap + 1) * per_group]) for tap in range(3)
    ]
    by_signal = jnp.concatenate([tn(pick, part).astype(BF16) for part in by_group], axis=0)
    by_group = jnp.concatenate(by_group, axis=0)
    head_matrix = block_diagonal(head_all)
    signal = lax.dynamic_slice_in_dim(signal_matrix, var_index * time_rows, time_rows, 0)
    signal = signal.reshape(-1, variates)
    marks = lax.dynamic_slice_in_dim(frame_numbers, var_index * time_rows, time_rows, 0)
    flags = window_flags(marks)
    marks_row = marks.astype(F32).reshape(time_rows, 1, length)
    since_a = blocks_since_start(marks, SA, iso_a.shape[0] // width)
    since_b = blocks_since_start(marks, SB, iso_b.shape[0] // width)

    trend, seasonal = front(signal, flags, marks_row, by_signal, length)
    lifted_a, act_a, second_a, joined_a = scale_forward(
        seasonal, down_a, iso_a, up_a, since_a, norm_gains, SA
    )
    lifted_b, act_b, second_b, joined_b = scale_forward(
        seasonal, down_b, iso_b, up_b, since_b, norm_gains, SB
    )
    (
        predicted, pre_a, pre_b, sres, merge_parts, ff_in_parts, ff_out_parts, head_full, gains_late,
    ) = tail(
        lifted_a, lifted_b, seasonal, trend, cotangent, merge_weight, ff_in, ff_out,
        head_matrix, norm_gains, length,
    )
    up_a_parts = up_grad(joined_a, pre_a)
    up_b_parts = up_grad(joined_b, pre_b)
    iso_pre_a, down_pre_a, block_a, gain_a = scale_backward(
        pre_a, up_a, iso_a, down_a, act_a, second_a, since_a, norm_gains
    )
    iso_pre_b, down_pre_b, block_b, gain_b = scale_backward(
        pre_b, up_b, iso_b, down_b, act_b, second_b, since_b, norm_gains
    )
    iso_a_parts = iso_grad(iso_pre_a, act_a, since_a, iso_a.shape[0] // width)
    iso_b_parts = iso_grad(iso_pre_b, act_b, since_b, iso_b.shape[0] // width)
    down_a_parts = down_grad(down_pre_a, seasonal)
    down_b_parts = down_grad(down_pre_b, seasonal)
    series_grad, embed_full = back(
        sres, block_a, block_b, cotangent, head_matrix, signal, flags, marks_row, by_group, length
    )
    gains_grad = jnp.concatenate([gains_late[0:1] + gain_a + gain_b, gains_late[1:]], axis=0)
    embed_full = jnp.einsum(
        "cv,tvd->tcd", pick.astype(F32), embed_full.reshape(3, variates, width),
        precision=lax.Precision.HIGHEST,
    )
    embed_grad = jnp.concatenate([diagonal_blocks(embed_full[tap], groups) for tap in range(3)], 1)
    head_grad = diagonal_blocks(head_full, groups)
    outward = jnp.stack([predicted, series_grad]).reshape(2, time_rows, length, variates)
    outward = lax.all_to_all(outward, "var", split_axis=3, concat_axis=1, tiled=True)
    embed_sum, head_sum, gains_sum = lax.psum((embed_grad, head_grad, gains_grad), ("rows", "var"))
    embed_sum = lax.dynamic_slice_in_dim(embed_sum, var_index * local_groups, local_groups, 0)
    head_sum = lax.dynamic_slice_in_dim(head_sum, var_index * local_groups, local_groups, 0)

    def shard(weight):
        return (weight.shape[0] // rows, weight.shape[1] // columns)

    summed = (
        scatter_sum(down_a_parts, True, across_first, shard(down_a)),
        scatter_sum(iso_a_parts, True, rows_first, shard(iso_a)),
        scatter_sum(up_a_parts, False, across_first, shard(up_a)),
        scatter_sum(down_b_parts, True, rows_first, shard(down_b)),
        scatter_sum(iso_b_parts, True, across_first, shard(iso_b)),
        scatter_sum(up_b_parts, False, rows_first, shard(up_b)),
        scatter_sum(merge_parts, True, across_first, shard(merge_weight)),
        scatter_sum(ff_in_parts, False, rows_first, shard(ff_in)),
        scatter_sum(ff_out_parts, True, across_first, shard(ff_out)),
    )
    return (outward[0], outward[1], embed_sum, head_sum, *summed, gains_sum)


def solution(mesh):
    placed = (
        P("rows", None, None),
        P("rows", None),
        P(),
        P("var", None, None),
        P("var", None, None),
        P(),
        P(),
        P(),
        P(),
        P(),
        P(),
        P(),
        P(),
        P(),
        P(),
        P("rows", None, "var"),
    )
    return jax.shard_map(
        body,
        mesh=mesh,
        in_specs=placed,
        out_specs=(
            P("rows", None, "var"),
            P("rows", None, "var"),
            P("var", None, None),
            P("var", None, None),
            P("rows", "var"),
            P("rows", "var"),
            P("rows", "var"),
            P("rows", "var"),
            P("rows", "var"),
            P("rows", "var"),
            P("rows", "var"),
            P("rows", "var"),
            P("rows", "var"),
            P(),
        ),
        check_vma=False,
    )
```

```python
import functools

import jax
import jax.numpy as jnp
from jax import lax
from jax.experimental import pallas as pl
from jax.experimental.pallas import tpu as pltpu
from jax.sharding import PartitionSpec as P

SA = 12
SB = 16
F32 = jnp.float32
BF16 = jnp.bfloat16
VMEM_LIMIT = 60 * 1024 * 1024


def nn(left, right):
    return lax.dot_general(left, right, (((1,), (0,)), ((), ())), preferred_element_type=F32)


def nt(left, right):
    return lax.dot_general(left, right, (((1,), (1,)), ((), ())), preferred_element_type=F32)


def tn(left, right):
    return lax.dot_general(left, right, (((0,), (0,)), ((), ())), preferred_element_type=F32)


def flip(values):
    return values.astype(F32).T.astype(BF16)


LANES = 128
ROW_PARTS = 8
COLUMN_PARTS = 4
ORDERS = {
    "x": ("x", "y", "near", "far"),
    "y": ("y", "near", "x", "far"),
    "z": ("near", "x", "y", "far"),
}


def part_at(order, r, x):
    place = {"far": r // 4, "near": r // 2 % 2, "y": r % 2, "x": x}
    return tuple(place[label] for label in ORDERS[order])


def from_part_order(values, order):
    labels = ("far", "near", "y", "x")
    places = [ORDERS[order].index(label) for label in labels]
    back = values.transpose(*places, *range(4, values.ndim))
    return back.reshape(8, 2, *values.shape[4:])


def picked(ref, rows):
    return jnp.concatenate([ref[c, rows, :] for c in range(ref.shape[0])], axis=1)


def placed(ref, rows, values):
    for c in range(ref.shape[0]):
        ref[c, rows, :] = values[:, c * LANES : (c + 1) * LANES]


def norm_parts(values):
    centre = values - jnp.mean(values, axis=-1, keepdims=True)
    spread = jnp.mean(centre * centre, axis=-1, keepdims=True)
    scale = lax.rsqrt(spread + 1e-05)
    return centre * scale, scale


def norm_back(grad, unit, scale, gain):
    inner = grad * gain
    first = jnp.mean(inner, axis=-1, keepdims=True)
    second = jnp.mean(inner * unit, axis=-1, keepdims=True)
    return (inner - first - unit * second) * scale, jnp.sum(grad * unit, axis=0, keepdims=True)


def gelu_pair(values):
    size = jnp.abs(values)
    bell = jnp.exp(values * values * -0.5)
    t = 1.0 / (1.0 + size * (0.3275911 * 0.7071067811865476))
    series = t * (
        0.127414796
        + t * (-0.142248368 + t * (0.7107068705 + t * (-0.7265760135 + t * 0.5307027145)))
    )
    tail = series * bell
    below = jnp.where(values >= 0.0, 1.0 - tail, tail)
    return values * below, below + values * bell * 0.3989422804014327


def bands(marks_column, marks_row, row_start, column_start):
    height, width = marks_column.shape[0], marks_row.shape[1]
    here = lax.broadcasted_iota(jnp.int32, (height, width), 0) + row_start
    there = lax.broadcasted_iota(jnp.int32, (height, width), 1) + column_start
    gap = jnp.abs(here - there)
    same = marks_column == marks_row
    near = jnp.where(jnp.logical_and(same, gap <= 6), 1.0, 0.0).astype(BF16)
    wide = jnp.where(jnp.logical_and(same, gap <= 8), 1.0, 0.0).astype(BF16)
    return near, wide


def tiles_of(length):
    tile, span = 256, 512
    return [(at, min(max(at - 128, 0), length - span), tile, span) for at in range(0, length, tile)]


def front_kernel(signal_ref, flags_ref, marks_ref, weight_ref, trend_ref, seasonal_ref, hidden_ref):
    length = signal_ref.shape[0]
    variates = signal_ref.shape[1]
    signal = signal_ref[...].astype(F32)
    before = (pltpu.roll(signal, 1, 0) * flags_ref[:, 0:1]).astype(BF16)
    after = (pltpu.roll(signal, length - 1, 0) * flags_ref[:, 1:2]).astype(BF16)
    hidden = nn(before, weight_ref[0:variates, :])
    hidden = hidden + nn(signal_ref[...], weight_ref[variates : 2 * variates, :])
    hidden = hidden + nn(after, weight_ref[2 * variates : 3 * variates, :])
    hidden_ref[...] = hidden.astype(BF16)
    for at, low, tile, span in tiles_of(length):
        near, wide = bands(
            flags_ref[at : at + tile, 4:5], marks_ref[0, :, low : low + span], at, low
        )
        source = hidden_ref[low : low + span, :]
        trend = nn(near, source) * flags_ref[at : at + tile, 2:3]
        trend = trend + nn(wide, source) * flags_ref[at : at + tile, 3:4]
        trend_ref[at : at + tile, :] = trend
        placed(seasonal_ref, slice(at, at + tile), hidden_ref[at : at + tile, :].astype(F32) - trend)


def front(signal, flags, marks_row, weight, length):
    positions, variates = signal.shape
    width = weight.shape[1]
    whole = lambda shape: pl.BlockSpec(shape, lambda i: (0,) * len(shape))
    return pl.pallas_call(
        front_kernel,
        grid=(positions // length,),
        in_specs=[
            pl.BlockSpec((length, variates), lambda i: (i, 0)),
            pl.BlockSpec((length, flags.shape[1]), lambda i: (i, 0)),
            pl.BlockSpec((1, 1, length), lambda i: (i, 0, 0)),
            whole(weight.shape),
        ],
        out_specs=[
            pl.BlockSpec((length, width), lambda i: (i, 0)),
            pl.BlockSpec((width // LANES, length, LANES), lambda i: (0, i, 0)),
        ],
        out_shape=[
            jax.ShapeDtypeStruct((positions, width), F32),
            jax.ShapeDtypeStruct((width // LANES, positions, LANES), F32),
        ],
        scratch_shapes=[pltpu.VMEM((length, width), BF16)],
        compiler_params=pltpu.CompilerParams(vmem_limit_bytes=VMEM_LIMIT),
        name="front",
    )(signal, flags, marks_row, weight)


def scale_forward_kernel(
    stride, taps, step_taps,
    seasonal_ref, down_ref, iso_ref, up_ref, since_ref, gain_ref,
    lifted_ref, act_ref, second_ref, joined_ref,
    total,
):
    step = pl.program_id(0)
    blocks, width = act_ref.shape
    down_steps, iso_steps = stride // step_taps, taps // step_taps

    @pl.when(step == 0)
    def _():
        total[...] = jnp.zeros_like(total)

    @pl.when(step < down_steps)
    def _():
        sums = total[...]
        for k in range(step_taps):
            rows = picked(seasonal_ref, pl.ds(step * step_taps + k, blocks, stride=stride))
            sums = sums + nn(rows.astype(BF16), down_ref[k * width : (k + 1) * width, :])
        total[...] = sums

    @pl.when(step == down_steps - 1)
    def _():
        active = jnp.tanh(total[...])
        act_ref[...] = active
        total[...] = jnp.zeros_like(total)

    @pl.when(jnp.logical_and(step >= down_steps, step < down_steps + iso_steps))
    def _():
        sums = total[...]
        for k in range(step_taps):
            back = taps - 1 - ((step - down_steps) * step_taps + k)
            rows = pltpu.roll(act_ref[...], back, 0)
            rows = jnp.where(since_ref[...] >= back, rows, 0.0).astype(BF16)
            sums = sums + nn(rows, iso_ref[k * width : (k + 1) * width, :])
        total[...] = sums

    @pl.when(step == down_steps + iso_steps - 1)
    def _():
        second = jnp.tanh(total[...])
        second_ref[...] = second
        unit, _ = norm_parts(second + act_ref[...])
        joined_ref[...] = (unit * gain_ref[0:1, :]).astype(BF16)

    @pl.when(step >= down_steps + iso_steps)
    def _():
        for k in range(step_taps):
            lifted = nn(joined_ref[...], up_ref[:, k * width : (k + 1) * width])
            lifted_ref[k] = jnp.tanh(lifted).astype(BF16)


def scale_forward(seasonal, down, iso, up, since, gains, stride):
    width, positions = down.shape[1], seasonal.shape[1]
    blocks = positions // stride
    taps = iso.shape[0] // width
    step_taps = 2
    ds, isteps = stride // step_taps, taps // step_taps
    whole = lambda shape: pl.BlockSpec(
        shape, lambda t: (0,) * len(shape), pipeline_mode=pl.Buffered(1)
    )
    clip = lambda value, top: jnp.minimum(jnp.maximum(value, 0), top)
    return pl.pallas_call(
        functools.partial(scale_forward_kernel, stride, taps, step_taps),
        grid=(2 * ds + isteps,),
        in_specs=[
            whole(seasonal.shape),
            pl.BlockSpec((step_taps * width, width), lambda t: (clip(t, ds - 1), 0)),
            pl.BlockSpec((step_taps * width, width), lambda t: (clip(t - ds, isteps - 1), 0)),
            pl.BlockSpec((width, step_taps * width), lambda t: (0, clip(t - ds - isteps, ds - 1))),
            whole(since.shape),
            whole(gains.shape),
        ],
        out_specs=[
            pl.BlockSpec(
                (step_taps, blocks, width), lambda t: (clip(t - ds - isteps, ds - 1), 0, 0)
            ),
            pl.BlockSpec((blocks, width), lambda t: (0, 0)),
            pl.BlockSpec((blocks, width), lambda t: (0, 0)),
            pl.BlockSpec((blocks, width), lambda t: (0, 0)),
        ],
        out_shape=[
            jax.ShapeDtypeStruct((stride, blocks, width), BF16),
            jax.ShapeDtypeStruct((blocks, width), F32),
            jax.ShapeDtypeStruct((blocks, width), F32),
            jax.ShapeDtypeStruct((blocks, width), BF16),
        ],
        scratch_shapes=[pltpu.VMEM((blocks, width), F32)],
        compiler_params=pltpu.CompilerParams(vmem_limit_bytes=VMEM_LIMIT),
        name="scale_forward",
    )(seasonal, down, iso, up, since, gains)


def tail_kernel(
    lifted_a_ref, lifted_b_ref, seasonal_ref, trend_ref, cot_ref,
    merge_ref, ff_in_ref, ff_out_ref, head_ref, gains_ref, mine_ref,
    pred_ref, up_a_ref, up_b_ref, sres_ref,
    parts_out, head_out, gains_out,
    wide_a, wide_b, inner_all, pre_all, slope, mixed_all, outer_all, merged_all, stacked_all,
    result_all, merge_sum, ff_in_sum, ff_out_sum,
):
    row = pl.program_id(0)
    length, width = trend_ref.shape
    hidden = ff_in_ref.shape[1]
    tile, chunk = 256, 512
    stride_a, per_a = lifted_a_ref.shape[0], lifted_a_ref.shape[1]
    stride_b, per_b = lifted_b_ref.shape[0], lifted_b_ref.shape[1]

    @pl.when(row == 0)
    def _():
        merge_sum[...] = jnp.zeros_like(merge_sum)
        ff_in_sum[...] = jnp.zeros_like(ff_in_sum)
        ff_out_sum[...] = jnp.zeros_like(ff_out_sum)
        head_out[...] = jnp.zeros_like(head_out)
        gains_out[...] = jnp.zeros_like(gains_out)

    for j in range(stride_a):
        placed(wide_a, pl.ds(j, per_a, stride=stride_a), lifted_a_ref[j].astype(F32))
    for j in range(stride_b):
        placed(wide_b, pl.ds(j, per_b, stride=stride_b), lifted_b_ref[j].astype(F32))
    gain_0, gain_1, gain_2 = gains_ref[0:1, :], gains_ref[1:2, :], gains_ref[2:3, :]

    def part(at, carry):
        rows = pl.ds(pl.multiple_of(at * tile, tile), tile)
        seasonal = picked(seasonal_ref, rows)
        unit_a, scale_a = norm_parts(picked(wide_a, rows) + seasonal)
        unit_b, scale_b = norm_parts(picked(wide_b, rows) + seasonal)
        branch_a = (unit_a * gain_0).astype(BF16)
        branch_b = (unit_b * gain_0).astype(BF16)
        stacked_all[rows, 0:width] = branch_a
        stacked_all[rows, width : 2 * width] = branch_b
        merged = nn(branch_a, merge_ref[0:width, :]) + nn(branch_b, merge_ref[width:, :])
        unit_1, scale_1 = norm_parts(merged)
        mixed = unit_1 * gain_1
        mixed_low = mixed.astype(BF16)
        mixed_all[rows, :] = mixed_low
        total = mixed
        for c in range(0, hidden, chunk):
            inner, fall = gelu_pair(nn(mixed_low, ff_in_ref[:, c : c + chunk]))
            inner_low = inner.astype(BF16)
            inner_all[rows, c : c + chunk] = inner_low
            slope[:, c : c + chunk] = fall.astype(BF16)
            total = total + nn(inner_low, ff_out_ref[c : c + chunk, :])
        unit_2, scale_2 = norm_parts(total)
        result_low = (unit_2 * gain_2 + trend_ref[rows, :]).astype(BF16)
        result_all[rows, :] = result_low
        pred_ref[rows, :] = nn(result_low, head_ref[...])
        result_grad = nt(cot_ref[rows, :], head_ref[...]).astype(BF16).astype(F32)
        final_grad, gain_grad_2 = norm_back(result_grad, unit_2, scale_2, gain_2)
        outer_low = final_grad.astype(BF16)
        outer_all[rows, :] = outer_low
        mixed_grad = final_grad
        for c in range(0, hidden, chunk):
            back = nt(outer_low, ff_out_ref[c : c + chunk, :])
            pre_low = (back * slope[:, c : c + chunk].astype(F32)).astype(BF16)
            pre_all[rows, c : c + chunk] = pre_low
            mixed_grad = mixed_grad + nt(pre_low, ff_in_ref[:, c : c + chunk])
        merged_grad, gain_grad_1 = norm_back(mixed_grad, unit_1, scale_1, gain_1)
        merged_low = merged_grad.astype(BF16)
        merged_all[rows, :] = merged_low
        lifted_a_grad, gain_grad_a = norm_back(
            nt(merged_low, merge_ref[0:width, :]), unit_a, scale_a, gain_0
        )
        lifted_b_grad, gain_grad_b = norm_back(
            nt(merged_low, merge_ref[width:, :]), unit_b, scale_b, gain_0
        )
        sres_ref[rows, :] = lifted_a_grad + lifted_b_grad
        value = picked(wide_a, rows)
        placed(wide_a, rows, lifted_a_grad * (1.0 - value * value))
        value = picked(wide_b, rows)
        placed(wide_b, rows, lifted_b_grad * (1.0 - value * value))
        gains_out[0:1, :] += gain_grad_a + gain_grad_b
        gains_out[1:2, :] += gain_grad_1
        gains_out[2:3, :] += gain_grad_2
        return carry

    lax.fori_loop(0, length // tile, part, 0)
    for j in range(stride_a):
        up_a_ref[j] = picked(wide_a, pl.ds(j, per_a, stride=stride_a)).astype(BF16)
    for j in range(stride_b):
        up_b_ref[j] = picked(wide_b, pl.ds(j, per_b, stride=stride_b)).astype(BF16)
    mixed_t, outer_t, merged_t = flip(mixed_all[...]), flip(outer_all[...]), flip(merged_all[...])
    for c in range(0, hidden, chunk):
        ff_in_sum[:, c : c + chunk] += nn(mixed_t, pre_all[:, c : c + chunk])
        ff_out_sum[:, c : c + chunk] += nn(outer_t, inner_all[:, c : c + chunk])
    for c in range(0, 2 * width, chunk):
        merge_sum[:, c : c + chunk] += nn(merged_t, stacked_all[:, c : c + chunk])
    head_out[...] += tn(result_all[...], cot_ref[...])

    @pl.when(row == pl.num_programs(0) - 1)
    def _():
        height = width // ROW_PARTS
        merge_size, out_size = 2 * width // ROW_PARTS, hidden // ROW_PARTS

        def store(r, carry):
            far, near, y = r // 4, r // 2 % 2, r % 2
            for v in range(COLUMN_PARTS):
                x, core = divmod(v, 2)
                side = jnp.where(mine_ref[0] == core, 0, 1)
                lines = slice(v * LANES, (v + 1) * LANES)
                blocks = []
                for p in range(merge_size // LANES):
                    low = pl.multiple_of(r * merge_size + p * LANES, LANES)
                    blocks.append(merge_sum[lines, pl.ds(low, LANES)])
                for p in range(hidden // (COLUMN_PARTS * LANES)):
                    low = v * (hidden // COLUMN_PARTS) + p * LANES
                    there = pl.ds(pl.multiple_of(r * height, height), height)
                    blocks.append(ff_in_sum[there, low : low + LANES])
                for p in range(out_size // LANES):
                    low = pl.multiple_of(r * out_size + p * LANES, LANES)
                    blocks.append(ff_out_sum[lines, pl.ds(low, LANES)])
                at = 0
                for block in blocks:
                    parts_out[side, near, x, y, far, at : at + block.shape[0], :] = block.astype(BF16)
                    at += block.shape[0]
            return carry

        lax.fori_loop(0, ROW_PARTS, store, 0)


def tail(
    lifted_a, lifted_b, seasonal, trend, cot, merge, ff_in, ff_out, head, gains, mine, length
):
    positions, width = trend.shape
    hidden = ff_in.shape[1]
    outs = cot.shape[1]
    stride_a, stride_b = lifted_a.shape[0], lifted_b.shape[0]
    per_a, per_b = length // stride_a, length // stride_b
    fixed = lambda shape: pl.BlockSpec(
        shape, lambda i: (0,) * len(shape), pipeline_mode=pl.Buffered(1)
    )
    kept = lambda shape: pl.BlockSpec(shape, lambda i: (0,) * len(shape))
    by_row = lambda size: pl.BlockSpec((length, size), lambda i: (i, 0))
    by_tap = lambda taps, per: pl.BlockSpec((taps, per, width), lambda i: (0, i, 0))
    lines = width * (2 * width + 2 * hidden) // (ROW_PARTS * COLUMN_PARTS * LANES)
    parts = (2, 2, 2, 2, 2, lines, LANES)
    return pl.pallas_call(
        tail_kernel,
        grid=(positions // length,),
        in_specs=[
            by_tap(stride_a, per_a), by_tap(stride_b, per_b),
            pl.BlockSpec((width // LANES, length, LANES), lambda i: (0, i, 0)), by_row(width),
            by_row(outs), fixed(merge.shape), fixed(ff_in.shape), fixed(ff_out.shape),
            fixed(head.shape), fixed(gains.shape), pl.BlockSpec(memory_space=pltpu.SMEM),
        ],
        out_specs=[
            by_row(outs), by_tap(stride_a, per_a), by_tap(stride_b, per_b), by_row(width),
            fixed(parts), kept((width, outs)), kept(gains.shape),
        ],
        out_shape=[
            jax.ShapeDtypeStruct((positions, outs), F32),
            jax.ShapeDtypeStruct(lifted_a.shape, BF16),
            jax.ShapeDtypeStruct(lifted_b.shape, BF16),
            jax.ShapeDtypeStruct((positions, width), F32),
            jax.ShapeDtypeStruct(parts, BF16),
            jax.ShapeDtypeStruct((width, outs), F32),
            jax.ShapeDtypeStruct(gains.shape, F32),
        ],
        scratch_shapes=[
            pltpu.VMEM((width // LANES, length, LANES), F32),
            pltpu.VMEM((width // LANES, length, LANES), F32),
            pltpu.VMEM((length, hidden), BF16), pltpu.VMEM((length, hidden), BF16),
            pltpu.VMEM((256, hidden), BF16), pltpu.VMEM((length, width), BF16),
            pltpu.VMEM((length, width), BF16), pltpu.VMEM((length, width), BF16),
            pltpu.VMEM((length, 2 * width), BF16), pltpu.VMEM((length, width), BF16),
            pltpu.VMEM((width, 2 * width), F32), pltpu.VMEM((width, hidden), F32),
            pltpu.VMEM((width, hidden), F32),
        ],
        compiler_params=pltpu.CompilerParams(vmem_limit_bytes=VMEM_LIMIT),
        name="tail",
    )(lifted_a, lifted_b, seasonal, trend, cot, merge, ff_in, ff_out, head, gains, mine)


def scale_backward_kernel(
    stride, taps, step_taps,
    pre_ref, up_ref, iso_ref, down_ref, act_ref, second_ref, since_ref, gain_ref,
    iso_pre_ref, down_pre_ref, block_ref, gain_out,
    total, spread,
):
    step = pl.program_id(0)
    blocks, width = act_ref.shape
    up_steps, iso_steps = stride // step_taps, taps // step_taps

    @pl.when(step == 0)
    def _():
        total[...] = jnp.zeros_like(total)
        spread[...] = jnp.zeros_like(spread)

    @pl.when(step < up_steps)
    def _():
        sums = total[...]
        for k in range(step_taps):
            sums = sums + nt(pre_ref[k], up_ref[:, k * width : (k + 1) * width])
        total[...] = sums

    @pl.when(step == up_steps - 1)
    def _():
        second = second_ref[...]
        unit, scale = norm_parts(second + act_ref[...])
        sum_grad, gain_grad = norm_back(total[...], unit, scale, gain_ref[0:1, :])
        gain_out[...] = gain_grad
        iso_pre_ref[...] = (sum_grad * (1.0 - second * second)).astype(BF16)
        spread[...] = sum_grad

    @pl.when(jnp.logical_and(step >= up_steps, step < up_steps + iso_steps))
    def _():
        for k in range(step_taps):
            back = taps - 1 - ((step - up_steps) * step_taps + k)
            grad = nt(iso_pre_ref[...], iso_ref[k * width : (k + 1) * width, :])
            grad = jnp.where(since_ref[...] >= back, grad, 0.0)
            spread[...] += pltpu.roll(grad, blocks - back, 0)

    @pl.when(step == up_steps + iso_steps - 1)
    def _():
        active = act_ref[...]
        down_pre_ref[...] = (spread[...] * (1.0 - active * active)).astype(BF16)

    @pl.when(step >= up_steps + iso_steps)
    def _():
        for k in range(step_taps):
            block_ref[k] = nt(
                down_pre_ref[...], down_ref[k * width : (k + 1) * width, :]
            ).astype(BF16)


def scale_backward(pre, up, iso, down, act, second, since, gains):
    stride, blocks, width = pre.shape
    taps = iso.shape[0] // width
    step_taps = 2
    us, isteps = stride // step_taps, taps // step_taps
    whole = lambda shape: pl.BlockSpec(
        shape, lambda t: (0,) * len(shape), pipeline_mode=pl.Buffered(1)
    )
    clip = lambda value, top: jnp.minimum(jnp.maximum(value, 0), top)
    return pl.pallas_call(
        functools.partial(scale_backward_kernel, stride, taps, step_taps),
        grid=(2 * us + isteps,),
        in_specs=[
            pl.BlockSpec((step_taps, blocks, width), lambda t: (clip(t, us - 1), 0, 0)),
            pl.BlockSpec((width, step_taps * width), lambda t: (0, clip(t, us - 1))),
            pl.BlockSpec((step_taps * width, width), lambda t: (clip(t - us, isteps - 1), 0)),
            pl.BlockSpec(
                (step_taps * width, width), lambda t: (clip(t - us - isteps, us - 1), 0)
            ),
            whole(act.shape), whole(second.shape), whole(since.shape), whole(gains.shape),
        ],
        out_specs=[
            pl.BlockSpec((blocks, width), lambda t: (0, 0)),
            pl.BlockSpec((blocks, width), lambda t: (0, 0)),
            pl.BlockSpec(
                (step_taps, blocks, width), lambda t: (clip(t - us - isteps, us - 1), 0, 0)
            ),
            pl.BlockSpec((1, width), lambda t: (0, 0)),
        ],
        out_shape=[
            jax.ShapeDtypeStruct((blocks, width), BF16),
            jax.ShapeDtypeStruct((blocks, width), BF16),
            jax.ShapeDtypeStruct((stride, blocks, width), BF16),
            jax.ShapeDtypeStruct((1, width), F32),
        ],
        scratch_shapes=[pltpu.VMEM((blocks, width), F32), pltpu.VMEM((blocks, width), F32)],
        compiler_params=pltpu.CompilerParams(vmem_limit_bytes=VMEM_LIMIT),
        name="scale_backward",
    )(pre, up, iso, down, act, second, since, gains)


def split_spec(grid, in_specs, out_specs, scratch):
    return pltpu.PrefetchScalarGridSpec(
        num_scalar_prefetch=1, grid=grid, in_specs=in_specs, out_specs=out_specs,
        scratch_shapes=scratch,
    )


def up_grad_kernel(order, mine_ref, own_joined, other_joined, own_pre, other_pre, out_ref, turned):
    blocks = own_joined.shape[0]

    @pl.when(jnp.logical_and(pl.program_id(0) == 0, pl.program_id(1) == 0))
    def _():
        turned[:, :blocks] = flip(own_joined[...])
        turned[:, blocks:] = flip(other_joined[...])

    rows = jnp.concatenate([own_pre[0], other_pre[0]], axis=0)
    product = nn(turned[...], rows).astype(BF16)
    panels, height, _ = out_ref.shape[4:]
    for r in range(ROW_PARTS):
        for p in range(panels):
            out_ref[(*part_at(order, r, 0), p)] = product[
                r * height : (r + 1) * height, p * LANES : (p + 1) * LANES
            ]


def up_grad(mine, joined, pre, order):
    stride, blocks, width = pre[0].shape
    taps, panels = stride // COLUMN_PARTS, width // LANES
    half = COLUMN_PARTS // 2
    height = width // ROW_PARTS
    sizes = tuple(1 if label == "x" else 2 for label in ORDERS[order])
    joined_spec = pl.BlockSpec((blocks, width), lambda x, j, mine: (0, 0))
    pre_spec = pl.BlockSpec(
        (1, blocks, width), lambda x, j, mine: ((2 * x + mine[0]) * taps + j, 0, 0)
    )
    return pl.pallas_call(
        functools.partial(up_grad_kernel, order),
        grid_spec=split_spec(
            (half, taps),
            [joined_spec, joined_spec, pre_spec, pre_spec],
            pl.BlockSpec(
                (*sizes, panels, height, LANES),
                lambda x, j, mine: (
                    *[x if label == "x" else 0 for label in ORDERS[order]], j, 0, 0
                ),
            ),
            [pltpu.VMEM((width, 2 * blocks), BF16)],
        ),
        out_shape=jax.ShapeDtypeStruct((2, 2, 2, 2, taps * panels, height, LANES), BF16),
        compiler_params=pltpu.CompilerParams(vmem_limit_bytes=VMEM_LIMIT),
        name="up_grad",
    )(mine, *joined, *pre)


def turn_half(turned, own_pre, other_pre, mine):
    blocks = own_pre.shape[0]
    for side, pre_ref in enumerate((own_pre, other_pre)):
        flipped = flip(pre_ref[...])
        there = slice(side * blocks, (side + 1) * blocks)
        for x in range(COLUMN_PARTS // 2):
            even = flipped[2 * x * LANES : (2 * x + 1) * LANES, :]
            odd = flipped[(2 * x + 1) * LANES : (2 * x + 2) * LANES, :]
            lines = slice(x * LANES, (x + 1) * LANES)

            @pl.when(mine == 0)
            def _(even=even, lines=lines, there=there):
                turned[lines, there] = even

            @pl.when(mine == 1)
            def _(odd=odd, lines=lines, there=there):
                turned[lines, there] = odd


def store_parts(orders, out_refs, k, product):
    per_part = out_refs[0].shape[4]
    panels = product.shape[1] // LANES
    for p in range(panels):
        r, at = divmod(panels * k + p, per_part * len(out_refs))
        piece, at = divmod(at, per_part)
        for x in range(COLUMN_PARTS // 2):
            out_refs[piece][(*part_at(orders[piece], r, x), at)] = product[
                x * LANES : (x + 1) * LANES, p * LANES : (p + 1) * LANES
            ]


GRAD_STEPS = 4


def grad_output(taps, width, order, pieces):
    per_part = taps * width // (ROW_PARTS * LANES * pieces)
    sizes = tuple(1 if label in ("near", "far") else 2 for label in ORDERS[order])
    spec = pl.BlockSpec(
        (*sizes, per_part, LANES, LANES),
        lambda t, mine: (
            *[{"near": t % 2, "far": t // 2}.get(label, 0) for label in ORDERS[order]], 0, 0, 0
        ),
    )
    return spec, jax.ShapeDtypeStruct((2, 2, 2, 2, per_part, LANES, LANES), BF16)


def grad_call(kernel, name, taps, width, blocks, orders, arguments, mine):
    whole = lambda shape: pl.BlockSpec(
        shape, lambda t, mine: (0,) * len(shape), pipeline_mode=pl.Buffered(1)
    )
    specs, shapes = zip(*[grad_output(taps, width, order, len(orders)) for order in orders])
    return pl.pallas_call(
        kernel,
        grid_spec=split_spec(
            (GRAD_STEPS,), [whole(value.shape) for value in arguments], list(specs),
            [pltpu.VMEM((width // 2, 2 * blocks), BF16)],
        ),
        out_shape=list(shapes),
        compiler_params=pltpu.CompilerParams(vmem_limit_bytes=VMEM_LIMIT),
        name=name,
    )(mine, *arguments)


def iso_grad_kernel(
    taps, orders, mine_ref, own_pre, other_pre, own_act, other_act, own_since, other_since, *rest
):
    *out_refs, turned = rest
    step = pl.program_id(0)
    step_taps = taps // GRAD_STEPS

    @pl.when(step == 0)
    def _():
        turn_half(turned, own_pre, other_pre, mine_ref[0])

    for k in range(step_taps):
        back = taps - 1 - (step * step_taps + k)
        rows = []
        for act_ref, since_ref in ((own_act, own_since), (other_act, other_since)):
            moved = pltpu.roll(act_ref[...], back, 0)
            rows.append(jnp.where(since_ref[...] >= back, moved, 0.0).astype(BF16))
        rows = jnp.concatenate(rows, axis=0)
        store_parts(orders, out_refs, k, nn(turned[...], rows).astype(BF16))


def iso_grad(mine, pre, act, since, taps, orders):
    blocks, width = act[0].shape
    kernel = functools.partial(iso_grad_kernel, taps, orders)
    return grad_call(
        kernel, "iso_grad", taps, width, blocks, orders, (*pre, *act, *since), mine
    )


def down_grad_kernel(
    stride, orders, mine_ref, own_pre, other_pre, own_seasonal, other_seasonal, *rest
):
    *out_refs, turned = rest
    step = pl.program_id(0)
    blocks = own_pre.shape[0]
    step_taps = stride // GRAD_STEPS

    @pl.when(step == 0)
    def _():
        turn_half(turned, own_pre, other_pre, mine_ref[0])

    for k in range(step_taps):
        there = pl.ds(step * step_taps + k, blocks, stride=stride)
        rows = [picked(ref, there).astype(BF16) for ref in (own_seasonal, other_seasonal)]
        rows = jnp.concatenate(rows, axis=0)
        store_parts(orders, out_refs, k, nn(turned[...], rows).astype(BF16))


def down_grad(mine, pre, seasonal, orders):
    blocks, width = pre[0].shape
    stride = seasonal[0].shape[1] // blocks
    kernel = functools.partial(down_grad_kernel, stride, orders)
    return grad_call(
        kernel, "down_grad", stride, width, blocks, orders, (*pre, *seasonal), mine
    )


def back_kernel(
    sres_ref, block_a_ref, block_b_ref, cot_ref, head_ref, signal_ref, flags_ref, marks_ref,
    weight_ref, series_ref, embed_ref, season, low_near, low_wide, hidden,
):
    length, width = sres_ref.shape
    variates = signal_ref.shape[1]
    stride_a, per_a = block_a_ref.shape[0], block_a_ref.shape[1]
    stride_b, per_b = block_b_ref.shape[0], block_b_ref.shape[1]

    @pl.when(pl.program_id(0) == 0)
    def _():
        embed_ref[...] = jnp.zeros_like(embed_ref)

    placed(season, slice(0, length), sres_ref[...])
    for j in range(stride_a):
        at = pl.ds(j, per_a, stride=stride_a)
        placed(season, at, picked(season, at) + block_a_ref[j].astype(F32))
    for j in range(stride_b):
        at = pl.ds(j, per_b, stride=stride_b)
        placed(season, at, picked(season, at) + block_b_ref[j].astype(F32))
    result_grad = nt(cot_ref[...], head_ref[...]).astype(BF16).astype(F32)
    gap = result_grad - picked(season, slice(0, length))
    low_near[...] = (gap * flags_ref[:, 2:3]).astype(BF16)
    low_wide[...] = (gap * flags_ref[:, 3:4]).astype(BF16)
    for at, low, tile, span in tiles_of(length):
        near, wide = bands(
            flags_ref[at : at + tile, 4:5], marks_ref[0, :, low : low + span], at, low
        )
        total = picked(season, slice(at, at + tile)) + nn(near, low_near[low : low + span, :])
        total = total + nn(wide, low_wide[low : low + span, :])
        hidden[at : at + tile, :] = total.astype(BF16)
    grad = hidden[...]
    first = nt(grad, weight_ref[0:variates, :]) * flags_ref[:, 0:1]
    last = nt(grad, weight_ref[2 * variates :, :]) * flags_ref[:, 1:2]
    series_ref[...] = (
        nt(grad, weight_ref[variates : 2 * variates, :])
        + pltpu.roll(first, length - 1, 0)
        + pltpu.roll(last, 1, 0)
    )
    signal = signal_ref[...].astype(F32)
    before = (pltpu.roll(signal, 1, 0) * flags_ref[:, 0:1]).astype(BF16)
    after = (pltpu.roll(signal, length - 1, 0) * flags_ref[:, 1:2]).astype(BF16)
    embed_ref[0:variates, :] += tn(before, grad)
    embed_ref[variates : 2 * variates, :] += tn(signal_ref[...], grad)
    embed_ref[2 * variates :, :] += tn(after, grad)


def back(sres, block_a, block_b, cot, head, signal, flags, marks_row, weight, length):
    positions, width = sres.shape
    variates = signal.shape[1]
    stride_a, stride_b = block_a.shape[0], block_b.shape[0]
    whole = lambda shape: pl.BlockSpec(shape, lambda i: (0,) * len(shape))
    by_row = lambda size: pl.BlockSpec((length, size), lambda i: (i, 0))
    return pl.pallas_call(
        back_kernel,
        grid=(positions // length,),
        in_specs=[
            by_row(width),
            pl.BlockSpec((stride_a, length // stride_a, width), lambda i: (0, i, 0)),
            pl.BlockSpec((stride_b, length // stride_b, width), lambda i: (0, i, 0)),
            by_row(cot.shape[1]), whole(head.shape), by_row(variates), by_row(flags.shape[1]),
            pl.BlockSpec((1, 1, length), lambda i: (i, 0, 0)), whole(weight.shape),
        ],
        out_specs=[by_row(variates), whole(weight.shape)],
        out_shape=[
            jax.ShapeDtypeStruct((positions, variates), F32),
            jax.ShapeDtypeStruct(weight.shape, F32),
        ],
        scratch_shapes=[
            pltpu.VMEM((width // LANES, length, LANES), F32), pltpu.VMEM((length, width), BF16),
            pltpu.VMEM((length, width), BF16), pltpu.VMEM((length, width), BF16),
        ],
        compiler_params=pltpu.CompilerParams(vmem_limit_bytes=VMEM_LIMIT),
        name="back",
    )(sres, block_a, block_b, cot, head, signal, flags, marks_row, weight)


def block_diagonal(pieces):
    count, height, width = pieces.shape
    eye = jnp.eye(count, dtype=pieces.dtype)
    spread = pieces[:, :, None, :] * eye[:, None, :, None]
    return spread.reshape(count * height, count * width)


def diagonal_blocks(matrix, count):
    height, width = matrix.shape[0] // count, matrix.shape[1] // count
    blocks = matrix.reshape(count, height, count, width)
    kept = jnp.eye(count, dtype=jnp.bool_)[:, None, :, None]
    return jnp.sum(jnp.where(kept, blocks, 0.0), axis=2)


def same_window(marks, offset):
    length = marks.shape[1]
    filler = jnp.full_like(marks[:, : abs(offset)], -1)
    if offset > 0:
        moved = jnp.concatenate([filler, marks[:, : length - offset]], axis=1)
    else:
        moved = jnp.concatenate([marks[:, -offset:], filler], axis=1)
    return (moved == marks).astype(F32)


def window_flags(marks):
    near = jnp.ones(marks.shape, F32)
    for offset in range(1, 7):
        near = near + same_window(marks, offset) + same_window(marks, -offset)
    wide = near
    for offset in range(7, 9):
        wide = wide + same_window(marks, offset) + same_window(marks, -offset)
    zero = jnp.zeros_like(near)
    columns = [
        same_window(marks, 1), same_window(marks, -1), 0.5 / near, 0.5 / wide,
        marks.astype(F32), zero, zero, zero,
    ]
    return jnp.stack(columns, axis=-1).reshape(-1, len(columns))


def blocks_since_start(marks, stride, taps):
    coarse = marks[:, ::stride]
    since = jnp.zeros(coarse.shape, F32)
    for offset in range(1, taps):
        since = since + same_window(coarse, offset)
    return since.astype(jnp.int32).reshape(-1, 1)


BITS = {"core": ("var", 0), "x": ("var", 1), "y": ("rows", 0), "near": ("rows", 1), "far": ("rows", 2)}


def own_bit(label):
    axis, bit = BITS[label]
    return (lax.axis_index(axis) >> bit) & 1


def cross(values, label):
    axis, bit = BITS[label]
    flipped = (1 << bit, 0) if axis == "rows" else (0, 1 << bit)
    pairs = [
        (r * COLUMN_PARTS + c, (r ^ flipped[0]) * COLUMN_PARTS + (c ^ flipped[1]))
        for r in range(ROW_PARTS)
        for c in range(COLUMN_PARTS)
    ]
    return lax.ppermute(values, ("rows", "var"), pairs)


class Turns:
    def __init__(self):
        self.last = ()

    def seen(self, *values):
        self.last = values

    def after(self, small):
        return lax.optimization_barrier((small, *self.last))[0]


class Halving:
    def __init__(self, turns, order):
        self.turns, self.left, self.order = turns, list(ORDERS[order]), order

    def start(self, *terms):
        self.lines = terms[0].size // (16 * LANES)
        self.terms = [term.reshape(-1, LANES) for term in terms]
        self.places = [jnp.int32(0)] * len(terms)

    def total(self, offset, lines):
        pieces = [
            lax.dynamic_slice(values, (place + offset, 0), (lines, LANES)).astype(F32)
            for values, place in zip(self.terms, self.places)
        ]
        return functools.reduce(jnp.add, pieces)

    def step(self):
        label = self.left.pop(0)
        lines = self.lines << len(self.left)
        mine = self.turns.after(own_bit(label))
        sent = self.total((1 - mine) * lines, lines).astype(BF16)
        self.turns.seen(sent)
        self.places = [place + mine * lines for place in self.places] + [jnp.int32(0)]
        self.terms.append(cross(sent, label))

    def finish(self):
        while self.left:
            self.step()
        return self.total(0, self.lines)


def by_columns(parts):
    return parts.reshape(-1, LANES, LANES).transpose(0, 2, 1).reshape(-1, LANES)


def by_features(parts, height):
    panels = parts.reshape(-1, height, LANES)
    return panels.transpose(1, 0, 2).reshape(height, -1)


def other_core(values):
    return lax.ppermute(
        values, "var", [(c, c ^ 1) for c in range(lax.axis_size("var"))]
    )


def both_halves(home, away, order, mine):
    home, away = from_part_order(home, order), from_part_order(away, order)
    first = jnp.where(mine == 0, home, away)
    second = jnp.where(mine == 0, away, home)
    halves = jnp.stack([first, second], axis=2)
    return halves.reshape(ROW_PARTS * COLUMN_PARTS, -1, LANES)


def scattered(full):
    rows, columns = lax.axis_size("rows"), lax.axis_size("var")
    height, depth = full.shape
    full = full.reshape(rows, height // rows, columns, depth // columns)
    full = full.transpose(0, 2, 1, 3).reshape(-1, depth // columns)
    return lax.psum_scatter(full, ("rows", "var"), scatter_dimension=0, tiled=True).astype(F32)


def scattered_columns(parts):
    width = COLUMN_PARTS * LANES
    panels = parts.reshape(ROW_PARTS, COLUMN_PARTS, -1, LANES, LANES)
    return scattered(panels.transpose(0, 2, 4, 1, 3).reshape(-1, width))


def scattered_features(parts, height):
    panels = parts.reshape(ROW_PARTS, COLUMN_PARTS, -1, height, LANES)
    return scattered(panels.transpose(0, 3, 1, 2, 4).reshape(ROW_PARTS * height, -1))


def sum_everywhere(values):
    for label in BITS:
        values = values + cross(values, label)
    return values


def body(
    signal_matrix, frame_numbers, variate_order, embed_weight, head_weight,
    down_a, iso_a, up_a, down_b, iso_b, up_b, merge_weight, ff_in, ff_out,
    norm_gains, estimate_cotangent,
):
    rows, columns = lax.axis_size("rows"), lax.axis_size("var")
    var_index = lax.axis_index("var")
    local_rows, length, variates = signal_matrix.shape
    local_groups = embed_weight.shape[0]
    per_group = head_weight.shape[2]
    groups = local_groups * columns
    time_rows = local_rows // columns
    width = norm_gains.shape[1]
    embed_all, head_all = lax.all_gather((embed_weight, head_weight), "var", axis=0, tiled=True)
    cotangent = lax.all_to_all(
        estimate_cotangent, "var", split_axis=0, concat_axis=2, tiled=True
    ).reshape(-1, variates)
    pick = jax.nn.one_hot(variate_order, variates, dtype=BF16)
    by_group = [
        block_diagonal(embed_all[:, tap * per_group : (tap + 1) * per_group]) for tap in range(3)
    ]
    by_signal = jnp.concatenate([tn(pick, part).astype(BF16) for part in by_group], axis=0)
    by_group = jnp.concatenate(by_group, axis=0)
    head_matrix = block_diagonal(head_all)
    signal = lax.dynamic_slice_in_dim(signal_matrix, var_index * time_rows, time_rows, 0)
    signal = signal.reshape(-1, variates)
    marks = lax.dynamic_slice_in_dim(frame_numbers, var_index * time_rows, time_rows, 0)
    flags = window_flags(marks)
    marks_row = marks.astype(F32).reshape(time_rows, 1, length)
    since_a = blocks_since_start(marks, SA, iso_a.shape[0] // width)
    since_b = blocks_since_start(marks, SB, iso_b.shape[0] // width)

    trend, seasonal = front(signal, flags, marks_row, by_signal, length)
    lifted_a, act_a, second_a, joined_a = scale_forward(
        seasonal, down_a, iso_a, up_a, since_a, norm_gains, SA
    )
    lifted_b, act_b, second_b, joined_b = scale_forward(
        seasonal, down_b, iso_b, up_b, since_b, norm_gains, SB
    )
    mixing = rows == ROW_PARTS and columns == COLUMN_PARTS
    mine = own_bit("core").reshape(1)
    pair = lambda values: (values, other_core(values))
    pair_marks = lax.dynamic_slice_in_dim(
        frame_numbers, (var_index ^ 1) * time_rows, time_rows, 0
    )
    since_a = (since_a, blocks_since_start(pair_marks, SA, iso_a.shape[0] // width))
    since_b = (since_b, blocks_since_start(pair_marks, SB, iso_b.shape[0] // width))
    seasonal_pair, act_pair_a, act_pair_b = pair(seasonal), pair(act_a), pair(act_b)
    joined_pair_a, joined_pair_b = pair(joined_a), pair(joined_b)
    predicted, pre_a, pre_b, sres, late_parts, head_full, gains_late = tail(
        lifted_a, lifted_b, seasonal, trend, cotangent, merge_weight, ff_in, ff_out,
        head_matrix, norm_gains, mine, length,
    )
    turns = Turns()
    orders = {
        "late": ("z",), "up_b": ("x",), "up_a": ("y",), "iso_a": ("z", "x"), "down_a": ("y",),
        "iso_b": ("x",), "down_b": ("y", "z"),
    }
    chains = {
        name: [Halving(turns, order) for order in pieces] for name, pieces in orders.items()
    }
    done = {}

    def go(*names):
        for name in names if mixing else ():
            for one in chains[name]:
                one.step()

    def produced(name, *pieces):
        done[name] = pieces
        turns.seen(*pieces)
        for one, piece in zip(chains[name], pieces):
            one.start(piece)

    def turn():
        return turns.after(mine)

    taps_a, taps_b = iso_a.shape[0] // width, iso_b.shape[0] // width
    turns.seen(late_parts)
    done["late"] = (late_parts,)
    if mixing:
        chains["late"][0].start(late_parts[0], cross(late_parts[1].reshape(-1, LANES), "core"))
    pre_pair_b, pre_pair_a = pair(pre_b), pair(pre_a)
    iso_pre_a, down_pre_a, block_a, gain_a = scale_backward(
        pre_a, up_a, iso_a, down_a, act_a, second_a, since_a[0], turns.after(norm_gains)
    )
    turns.seen(iso_pre_a)
    iso_pre_pair_a, down_pre_pair_a = pair(iso_pre_a), pair(down_pre_a)
    go("late")
    produced("up_b", up_grad(turn(), joined_pair_b, pre_pair_b, "x"))
    go("up_b")
    produced("up_a", up_grad(turn(), joined_pair_a, pre_pair_a, "y"))
    go("up_a")
    iso_pre_b, down_pre_b, block_b, gain_b = scale_backward(
        pre_b, up_b, iso_b, down_b, act_b, second_b, since_b[0], turns.after(norm_gains)
    )
    turns.seen(iso_pre_b)
    iso_pre_pair_b, down_pre_pair_b = pair(iso_pre_b), pair(down_pre_b)
    produced(
        "iso_a", *iso_grad(turn(), iso_pre_pair_a, act_pair_a, since_a, taps_a, orders["iso_a"])
    )
    produced("down_a", *down_grad(turn(), down_pre_pair_a, seasonal_pair, orders["down_a"]))
    go("late", "up_b", "up_a", "iso_a", "down_a")
    produced(
        "iso_b", *iso_grad(turn(), iso_pre_pair_b, act_pair_b, since_b, taps_b, orders["iso_b"])
    )
    produced("down_b", *down_grad(turn(), down_pre_pair_b, seasonal_pair, orders["down_b"]))
    go("late", "up_b", "up_a", "iso_b", "down_b")
    series_grad, embed_full = back(
        sres, block_a, block_b, cotangent, head_matrix, signal, flags, marks_row,
        turns.after(by_group), length
    )
    turns.seen(embed_full)
    gains_grad = jnp.concatenate([gains_late[0:1] + gain_a + gain_b, gains_late[1:]], axis=0)
    embed_full = jnp.einsum(
        "cv,tvd->tcd", pick.astype(F32), embed_full.reshape(3, variates, width),
        precision=lax.Precision.HIGHEST,
    )
    embed_grad = jnp.concatenate([diagonal_blocks(embed_full[tap], groups) for tap in range(3)], 1)
    head_grad = diagonal_blocks(head_full, groups)
    outward = jnp.stack([predicted, series_grad]).reshape(2, time_rows, length, variates)
    outward = lax.all_to_all(outward, "var", split_axis=3, concat_axis=1, tiled=True)
    small = (embed_grad, head_grad, gains_grad)
    if mixing:
        flat = sum_everywhere(jnp.concatenate([part.reshape(-1, LANES) for part in small]))
        pieces, at = [], 0
        for part in small:
            lines = part.size // LANES
            pieces.append(flat[at : at + lines].reshape(part.shape))
            at += lines
        embed_sum, head_sum, gains_sum = pieces
    else:
        embed_sum, head_sum, gains_sum = lax.psum(small, ("rows", "var"))
    embed_sum = lax.dynamic_slice_in_dim(embed_sum, var_index * local_groups, local_groups, 0)
    head_sum = lax.dynamic_slice_in_dim(head_sum, var_index * local_groups, local_groups, 0)

    height = width // ROW_PARTS
    merge_lines = merge_weight.size // (ROW_PARTS * COLUMN_PARTS * LANES)
    in_lines = ff_in.size // (ROW_PARTS * COLUMN_PARTS * LANES)
    if mixing:
        go("iso_a", "down_a", "late", "up_b", "up_a", "iso_b", "down_b")
        go("iso_a", "down_a", "iso_b", "down_b", "iso_a", "down_a", "iso_b", "down_b")
        total = {
            name: jnp.concatenate([one.finish() for one in pieces])
            for name, pieces in chains.items()
        }
        late = total["late"]
        turned, kept = by_columns, by_features
    else:
        total = {}
        for name, pieces in done.items():
            if name == "late":
                halves = [(pieces[0][0], pieces[0][1])]
            else:
                halves = [(piece, jnp.zeros_like(piece)) for piece in pieces]
            total[name] = jnp.concatenate(
                [both_halves(*two, order, mine[0]) for two, order in zip(halves, orders[name])],
                axis=1,
            )
        late = total["late"]
        turned, kept = scattered_columns, scattered_features
    split = (merge_lines, merge_lines + in_lines)
    merge_part, in_part, out_part = jnp.split(late, split, axis=late.ndim - 2)
    summed = (
        turned(total["down_a"]), turned(total["iso_a"]), kept(total["up_a"], height),
        turned(total["down_b"]), turned(total["iso_b"]), kept(total["up_b"], height),
        turned(merge_part), kept(in_part, height), turned(out_part),
    )
    return (outward[0], outward[1], embed_sum, head_sum, *summed, gains_sum)


def solution(mesh):
    placed = (
        P("rows", None, None),
        P("rows", None),
        P(),
        P("var", None, None),
        P("var", None, None),
        P(),
        P(),
        P(),
        P(),
        P(),
        P(),
        P(),
        P(),
        P(),
        P(),
        P("rows", None, "var"),
    )
    return jax.shard_map(
        body,
        mesh=mesh,
        in_specs=placed,
        out_specs=(
            P("rows", None, "var"),
            P("rows", None, "var"),
            P("var", None, None),
            P("var", None, None),
            P("rows", "var"),
            P("rows", "var"),
            P("rows", "var"),
            P("rows", "var"),
            P("rows", "var"),
            P("rows", "var"),
            P("rows", "var"),
            P("rows", "var"),
            P("rows", "var"),
            P(),
        ),
        check_vma=False,
    )
```

```python
import functools

import jax
import jax.numpy as jnp
from jax import lax
from jax.experimental import pallas as pl
from jax.experimental.pallas import tpu as pltpu
from jax.sharding import PartitionSpec as P

SA = 12
SB = 16
F32 = jnp.float32
BF16 = jnp.bfloat16
VMEM_LIMIT = 60 * 1024 * 1024


def nn(left, right):
    return lax.dot_general(left, right, (((1,), (0,)), ((), ())), preferred_element_type=F32)


def nt(left, right):
    return lax.dot_general(left, right, (((1,), (1,)), ((), ())), preferred_element_type=F32)


def tn(left, right):
    return lax.dot_general(left, right, (((0,), (0,)), ((), ())), preferred_element_type=F32)


def flip(values):
    return values.astype(F32).T.astype(BF16)


LANES = 128
STEP_TAPS = 4
ROW_PARTS = 8
COLUMN_PARTS = 4
ORDERS = {
    "xyn": ("x", "y", "near", "far"),
    "xny": ("x", "near", "y", "far"),
    "yxn": ("y", "x", "near", "far"),
    "ynx": ("y", "near", "x", "far"),
    "nxy": ("near", "x", "y", "far"),
    "nyx": ("near", "y", "x", "far"),
}


def part_at(order, r, x):
    place = {"far": r // 4, "near": r // 2 % 2, "y": r % 2, "x": x}
    return tuple(place[label] for label in ORDERS[order])


def from_part_order(values, order):
    labels = ("far", "near", "y", "x")
    places = [ORDERS[order].index(label) for label in labels]
    back = values.transpose(*places, *range(4, values.ndim))
    return back.reshape(8, 2, *values.shape[4:])


def picked(ref, rows):
    return jnp.concatenate([ref[c, rows, :] for c in range(ref.shape[0])], axis=1)


def placed(ref, rows, values):
    for c in range(ref.shape[0]):
        ref[c, rows, :] = values[:, c * LANES : (c + 1) * LANES]


def norm_parts(values):
    centre = values - jnp.mean(values, axis=-1, keepdims=True)
    spread = jnp.mean(centre * centre, axis=-1, keepdims=True)
    scale = lax.rsqrt(spread + 1e-05)
    return centre * scale, scale


def norm_back(grad, unit, scale, gain):
    inner = grad * gain
    first = jnp.mean(inner, axis=-1, keepdims=True)
    second = jnp.mean(inner * unit, axis=-1, keepdims=True)
    return (inner - first - unit * second) * scale, jnp.sum(grad * unit, axis=0, keepdims=True)


def gelu_pair(values):
    size = jnp.abs(values)
    bell = jnp.exp(values * values * -0.5)
    t = 1.0 / (1.0 + size * (0.3275911 * 0.7071067811865476))
    series = t * (
        0.127414796
        + t * (-0.142248368 + t * (0.7107068705 + t * (-0.7265760135 + t * 0.5307027145)))
    )
    tail = series * bell
    below = jnp.where(values >= 0.0, 1.0 - tail, tail)
    return values * below, below + values * bell * 0.3989422804014327


def bands(marks_column, marks_row, row_start, column_start):
    height, width = marks_column.shape[0], marks_row.shape[1]
    here = lax.broadcasted_iota(jnp.int32, (height, width), 0) + row_start
    there = lax.broadcasted_iota(jnp.int32, (height, width), 1) + column_start
    gap = jnp.abs(here - there)
    same = marks_column == marks_row
    near = jnp.where(jnp.logical_and(same, gap <= 6), 1.0, 0.0).astype(BF16)
    wide = jnp.where(jnp.logical_and(same, gap <= 8), 1.0, 0.0).astype(BF16)
    return near, wide


def tiles_of(length):
    tile, span = 256, 512
    return [(at, min(max(at - 128, 0), length - span), tile, span) for at in range(0, length, tile)]


def front_kernel(
    signal_ref, flags_ref, marks_ref, weight_ref, trend_ref, seasonal_ref, taps_a_ref, taps_b_ref,
    hidden_ref, lanes_ref,
):
    length = signal_ref.shape[0]
    variates = signal_ref.shape[1]
    signal = signal_ref[...].astype(F32)
    before = (pltpu.roll(signal, 1, 0) * flags_ref[:, 0:1]).astype(BF16)
    after = (pltpu.roll(signal, length - 1, 0) * flags_ref[:, 1:2]).astype(BF16)
    hidden = nn(before, weight_ref[0:variates, :])
    hidden = hidden + nn(signal_ref[...], weight_ref[variates : 2 * variates, :])
    hidden = hidden + nn(after, weight_ref[2 * variates : 3 * variates, :])
    hidden_ref[...] = hidden.astype(BF16)
    for at, low, tile, span in tiles_of(length):
        near, wide = bands(
            flags_ref[at : at + tile, 4:5], marks_ref[0, :, low : low + span], at, low
        )
        source = hidden_ref[low : low + span, :]
        trend = nn(near, source) * flags_ref[at : at + tile, 2:3]
        trend = trend + nn(wide, source) * flags_ref[at : at + tile, 3:4]
        trend_ref[at : at + tile, :] = trend
        seasonal = hidden_ref[at : at + tile, :].astype(F32) - trend
        seasonal_ref[at : at + tile, :] = seasonal
        placed(lanes_ref, slice(at, at + tile), seasonal)
    for taps_ref in (taps_a_ref, taps_b_ref):
        stride, blocks, _ = taps_ref.shape
        for j in range(stride):
            taps_ref[j] = picked(lanes_ref, pl.ds(j, blocks, stride=stride)).astype(BF16)


def front(signal, flags, marks_row, weight, length):
    positions, variates = signal.shape
    width = weight.shape[1]
    whole = lambda shape: pl.BlockSpec(shape, lambda i: (0,) * len(shape))
    return pl.pallas_call(
        front_kernel,
        grid=(positions // length,),
        in_specs=[
            pl.BlockSpec((length, variates), lambda i: (i, 0)),
            pl.BlockSpec((length, flags.shape[1]), lambda i: (i, 0)),
            pl.BlockSpec((1, 1, length), lambda i: (i, 0, 0)),
            whole(weight.shape),
        ],
        out_specs=[
            pl.BlockSpec((length, width), lambda i: (i, 0)),
            pl.BlockSpec((length, width), lambda i: (i, 0)),
            *[pl.BlockSpec((s, length // s, width), lambda i: (0, i, 0)) for s in (SA, SB)],
        ],
        out_shape=[
            jax.ShapeDtypeStruct((positions, width), F32),
            jax.ShapeDtypeStruct((positions, width), F32),
            *[jax.ShapeDtypeStruct((s, positions // s, width), BF16) for s in (SA, SB)],
        ],
        scratch_shapes=[
            pltpu.VMEM((length, width), BF16), pltpu.VMEM((width // LANES, length, LANES), F32),
        ],
        compiler_params=pltpu.CompilerParams(vmem_limit_bytes=VMEM_LIMIT),
        name="front",
    )(signal, flags, marks_row, weight)


def scale_forward_kernel(
    stride, taps, step_taps,
    seasonal_ref, down_ref, iso_ref, up_ref, since_ref, gain_ref,
    lifted_ref, act_ref, second_ref, joined_ref,
    total,
):
    step = pl.program_id(0)
    blocks, width = act_ref.shape
    down_steps, iso_steps = stride // step_taps, taps // step_taps

    @pl.when(step == 0)
    def _():
        total[...] = jnp.zeros_like(total)

    @pl.when(step < down_steps)
    def _():
        rows = jnp.concatenate([seasonal_ref[k] for k in range(step_taps)], axis=1)
        total[...] += nn(rows, down_ref[...])

    @pl.when(step == down_steps - 1)
    def _():
        active = jnp.tanh(total[...])
        act_ref[...] = active
        joined_ref[1] = active.astype(BF16)
        total[...] = jnp.zeros_like(total)

    @pl.when(jnp.logical_and(step >= down_steps, step < down_steps + iso_steps))
    def _():
        pieces = []
        for k in range(step_taps):
            back = taps - 1 - ((step - down_steps) * step_taps + k)
            rows = pltpu.roll(act_ref[...], back, 0)
            pieces.append(jnp.where(since_ref[...] >= back, rows, 0.0).astype(BF16))
        total[...] += nn(jnp.concatenate(pieces, axis=1), iso_ref[...])

    @pl.when(step == down_steps + iso_steps - 1)
    def _():
        second = jnp.tanh(total[...])
        second_ref[...] = second
        unit, _ = norm_parts(second + act_ref[...])
        joined_ref[0] = (unit * gain_ref[0:1, :]).astype(BF16)

    @pl.when(step >= down_steps + iso_steps)
    def _():
        for k in range(step_taps):
            lifted = nn(joined_ref[0], up_ref[:, k * width : (k + 1) * width])
            lifted_ref[k] = jnp.tanh(lifted).astype(BF16)


def scale_forward(seasonal, down, iso, up, since, gains, stride):
    _, blocks, width = seasonal.shape
    taps = iso.shape[0] // width
    step_taps = STEP_TAPS
    ds, isteps = stride // step_taps, taps // step_taps
    whole = lambda shape: pl.BlockSpec(
        shape, lambda t: (0,) * len(shape), pipeline_mode=pl.Buffered(1)
    )
    clip = lambda value, top: jnp.minimum(jnp.maximum(value, 0), top)
    return pl.pallas_call(
        functools.partial(scale_forward_kernel, stride, taps, step_taps),
        grid=(2 * ds + isteps,),
        in_specs=[
            pl.BlockSpec((step_taps, blocks, width), lambda t: (clip(t, ds - 1), 0, 0)),
            pl.BlockSpec((step_taps * width, width), lambda t: (clip(t, ds - 1), 0)),
            pl.BlockSpec((step_taps * width, width), lambda t: (clip(t - ds, isteps - 1), 0)),
            pl.BlockSpec((width, step_taps * width), lambda t: (0, clip(t - ds - isteps, ds - 1))),
            whole(since.shape),
            whole(gains.shape),
        ],
        out_specs=[
            pl.BlockSpec(
                (step_taps, blocks, width), lambda t: (clip(t - ds - isteps, ds - 1), 0, 0)
            ),
            pl.BlockSpec((blocks, width), lambda t: (0, 0)),
            pl.BlockSpec((blocks, width), lambda t: (0, 0)),
            pl.BlockSpec((2, blocks, width), lambda t: (0, 0, 0)),
        ],
        out_shape=[
            jax.ShapeDtypeStruct((stride, blocks, width), BF16),
            jax.ShapeDtypeStruct((blocks, width), F32),
            jax.ShapeDtypeStruct((blocks, width), F32),
            jax.ShapeDtypeStruct((2, blocks, width), BF16),
        ],
        scratch_shapes=[pltpu.VMEM((blocks, width), F32)],
        compiler_params=pltpu.CompilerParams(vmem_limit_bytes=VMEM_LIMIT),
        name="scale_forward",
    )(seasonal, down, iso, up, since, gains)


def tail_kernel(
    lifted_a_ref, lifted_b_ref, seasonal_ref, trend_ref, cot_ref,
    merge_ref, ff_in_ref, ff_out_ref, head_ref, gains_ref, mine_ref,
    pred_ref, up_a_ref, up_b_ref, sres_ref,
    parts_out, head_out, gains_out,
    wide_a, wide_b, inner_all, pre_all, slope, mixed_all, outer_all, merged_all, stacked_all,
    result_all, merge_sum, ff_in_sum, ff_out_sum,
):
    row = pl.program_id(0)
    length, width = trend_ref.shape
    hidden = ff_in_ref.shape[1]
    tile, chunk = 256, 512
    stride_a, per_a = lifted_a_ref.shape[0], lifted_a_ref.shape[1]
    stride_b, per_b = lifted_b_ref.shape[0], lifted_b_ref.shape[1]

    @pl.when(row == 0)
    def _():
        merge_sum[...] = jnp.zeros_like(merge_sum)
        ff_in_sum[...] = jnp.zeros_like(ff_in_sum)
        ff_out_sum[...] = jnp.zeros_like(ff_out_sum)
        head_out[...] = jnp.zeros_like(head_out)
        gains_out[...] = jnp.zeros_like(gains_out)

    for j in range(stride_a):
        placed(wide_a, pl.ds(j, per_a, stride=stride_a), lifted_a_ref[j].astype(F32))
    for j in range(stride_b):
        placed(wide_b, pl.ds(j, per_b, stride=stride_b), lifted_b_ref[j].astype(F32))
    gain_0, gain_1, gain_2 = gains_ref[0:1, :], gains_ref[1:2, :], gains_ref[2:3, :]

    def part(at, carry):
        rows = pl.ds(pl.multiple_of(at * tile, tile), tile)
        seasonal = seasonal_ref[rows, :]
        unit_a, scale_a = norm_parts(picked(wide_a, rows) + seasonal)
        unit_b, scale_b = norm_parts(picked(wide_b, rows) + seasonal)
        branch_a = (unit_a * gain_0).astype(BF16)
        branch_b = (unit_b * gain_0).astype(BF16)
        stacked_all[rows, 0:width] = branch_a
        stacked_all[rows, width : 2 * width] = branch_b
        merged = nn(branch_a, merge_ref[0:width, :]) + nn(branch_b, merge_ref[width:, :])
        unit_1, scale_1 = norm_parts(merged)
        mixed = unit_1 * gain_1
        mixed_low = mixed.astype(BF16)
        mixed_all[rows, :] = mixed_low
        total = mixed
        for c in range(0, hidden, chunk):
            inner, fall = gelu_pair(nn(mixed_low, ff_in_ref[:, c : c + chunk]))
            inner_low = inner.astype(BF16)
            inner_all[rows, c : c + chunk] = inner_low
            slope[:, c : c + chunk] = fall.astype(BF16)
            total = total + nn(inner_low, ff_out_ref[c : c + chunk, :])
        unit_2, scale_2 = norm_parts(total)
        result_low = (unit_2 * gain_2 + trend_ref[rows, :]).astype(BF16)
        result_all[rows, :] = result_low
        pred_ref[rows, :] = nn(result_low, head_ref[...])
        result_grad = nt(cot_ref[rows, :], head_ref[...]).astype(BF16).astype(F32)
        final_grad, gain_grad_2 = norm_back(result_grad, unit_2, scale_2, gain_2)
        outer_low = final_grad.astype(BF16)
        outer_all[rows, :] = outer_low
        mixed_grad = final_grad
        for c in range(0, hidden, chunk):
            back = nt(outer_low, ff_out_ref[c : c + chunk, :])
            pre_low = (back * slope[:, c : c + chunk].astype(F32)).astype(BF16)
            pre_all[rows, c : c + chunk] = pre_low
            mixed_grad = mixed_grad + nt(pre_low, ff_in_ref[:, c : c + chunk])
        merged_grad, gain_grad_1 = norm_back(mixed_grad, unit_1, scale_1, gain_1)
        merged_low = merged_grad.astype(BF16)
        merged_all[rows, :] = merged_low
        lifted_a_grad, gain_grad_a = norm_back(
            nt(merged_low, merge_ref[0:width, :]), unit_a, scale_a, gain_0
        )
        lifted_b_grad, gain_grad_b = norm_back(
            nt(merged_low, merge_ref[width:, :]), unit_b, scale_b, gain_0
        )
        sres_ref[rows, :] = lifted_a_grad + lifted_b_grad
        value = picked(wide_a, rows)
        placed(wide_a, rows, lifted_a_grad * (1.0 - value * value))
        value = picked(wide_b, rows)
        placed(wide_b, rows, lifted_b_grad * (1.0 - value * value))
        gains_out[0:1, :] += gain_grad_a + gain_grad_b
        gains_out[1:2, :] += gain_grad_1
        gains_out[2:3, :] += gain_grad_2
        return carry

    lax.fori_loop(0, length // tile, part, 0)
    for j in range(stride_a):
        up_a_ref[j] = picked(wide_a, pl.ds(j, per_a, stride=stride_a)).astype(BF16)
    for j in range(stride_b):
        up_b_ref[j] = picked(wide_b, pl.ds(j, per_b, stride=stride_b)).astype(BF16)
    mixed_t, outer_t, merged_t = flip(mixed_all[...]), flip(outer_all[...]), flip(merged_all[...])
    for c in range(0, hidden, chunk):
        ff_in_sum[:, c : c + chunk] += nn(mixed_t, pre_all[:, c : c + chunk])
        ff_out_sum[:, c : c + chunk] += nn(outer_t, inner_all[:, c : c + chunk])
    for c in range(0, 2 * width, chunk):
        merge_sum[:, c : c + chunk] += nn(merged_t, stacked_all[:, c : c + chunk])
    head_out[...] += tn(result_all[...], cot_ref[...])

    @pl.when(row == pl.num_programs(0) - 1)
    def _():
        height = width // ROW_PARTS
        merge_size, out_size = 2 * width // ROW_PARTS, hidden // ROW_PARTS

        def store(r, carry):
            far, near, y = r // 4, r // 2 % 2, r % 2
            for v in range(COLUMN_PARTS):
                x, core = divmod(v, 2)
                side = jnp.where(mine_ref[0] == core, 0, 1)
                lines = slice(v * LANES, (v + 1) * LANES)
                blocks = []
                for p in range(merge_size // LANES):
                    low = pl.multiple_of(r * merge_size + p * LANES, LANES)
                    blocks.append(merge_sum[lines, pl.ds(low, LANES)])
                for p in range(hidden // (COLUMN_PARTS * LANES)):
                    low = v * (hidden // COLUMN_PARTS) + p * LANES
                    there = pl.ds(pl.multiple_of(r * height, height), height)
                    blocks.append(ff_in_sum[there, low : low + LANES])
                for p in range(out_size // LANES):
                    low = pl.multiple_of(r * out_size + p * LANES, LANES)
                    blocks.append(ff_out_sum[lines, pl.ds(low, LANES)])
                at = 0
                for block in blocks:
                    parts_out[side, near, x, y, far, at : at + block.shape[0], :] = block.astype(BF16)
                    at += block.shape[0]
            return carry

        lax.fori_loop(0, ROW_PARTS, store, 0)


def tail(
    lifted_a, lifted_b, seasonal, trend, cot, merge, ff_in, ff_out, head, gains, mine, length
):
    positions, width = trend.shape
    hidden = ff_in.shape[1]
    outs = cot.shape[1]
    stride_a, stride_b = lifted_a.shape[0], lifted_b.shape[0]
    per_a, per_b = length // stride_a, length // stride_b
    fixed = lambda shape: pl.BlockSpec(
        shape, lambda i: (0,) * len(shape), pipeline_mode=pl.Buffered(1)
    )
    kept = lambda shape: pl.BlockSpec(shape, lambda i: (0,) * len(shape))
    by_row = lambda size: pl.BlockSpec((length, size), lambda i: (i, 0))
    by_tap = lambda taps, per: pl.BlockSpec((taps, per, width), lambda i: (0, i, 0))
    lines = width * (2 * width + 2 * hidden) // (ROW_PARTS * COLUMN_PARTS * LANES)
    parts = (2, 2, 2, 2, 2, lines, LANES)
    return pl.pallas_call(
        tail_kernel,
        grid=(positions // length,),
        in_specs=[
            by_tap(stride_a, per_a), by_tap(stride_b, per_b),
            by_row(width), by_row(width), by_row(outs), fixed(merge.shape), fixed(ff_in.shape), fixed(ff_out.shape),
            fixed(head.shape), fixed(gains.shape), pl.BlockSpec(memory_space=pltpu.SMEM),
        ],
        out_specs=[
            by_row(outs), by_tap(stride_a, per_a), by_tap(stride_b, per_b), by_row(width),
            fixed(parts), kept((width, outs)), kept(gains.shape),
        ],
        out_shape=[
            jax.ShapeDtypeStruct((positions, outs), F32),
            jax.ShapeDtypeStruct(lifted_a.shape, BF16),
            jax.ShapeDtypeStruct(lifted_b.shape, BF16),
            jax.ShapeDtypeStruct((positions, width), F32),
            jax.ShapeDtypeStruct(parts, BF16),
            jax.ShapeDtypeStruct((width, outs), F32),
            jax.ShapeDtypeStruct(gains.shape, F32),
        ],
        scratch_shapes=[
            pltpu.VMEM((width // LANES, length, LANES), F32),
            pltpu.VMEM((width // LANES, length, LANES), F32),
            pltpu.VMEM((length, hidden), BF16), pltpu.VMEM((length, hidden), BF16),
            pltpu.VMEM((256, hidden), BF16), pltpu.VMEM((length, width), BF16),
            pltpu.VMEM((length, width), BF16), pltpu.VMEM((length, width), BF16),
            pltpu.VMEM((length, 2 * width), BF16), pltpu.VMEM((length, width), BF16),
            pltpu.VMEM((width, 2 * width), F32), pltpu.VMEM((width, hidden), F32),
            pltpu.VMEM((width, hidden), F32),
        ],
        compiler_params=pltpu.CompilerParams(vmem_limit_bytes=VMEM_LIMIT),
        name="tail",
    )(lifted_a, lifted_b, seasonal, trend, cot, merge, ff_in, ff_out, head, gains, mine)


def scale_backward_kernel(
    stride, taps, step_taps,
    pre_ref, up_ref, iso_ref, down_ref, act_ref, second_ref, since_ref, gain_ref,
    both_pre_ref, block_ref, gain_out,
    total, spread,
):
    step = pl.program_id(0)
    blocks, width = act_ref.shape
    up_steps, iso_steps = stride // step_taps, taps // step_taps

    @pl.when(step == 0)
    def _():
        total[...] = jnp.zeros_like(total)
        spread[...] = jnp.zeros_like(spread)

    @pl.when(step < up_steps)
    def _():
        rows = jnp.concatenate([pre_ref[k] for k in range(step_taps)], axis=1)
        total[...] += nt(rows, up_ref[...])

    @pl.when(step == up_steps - 1)
    def _():
        second = second_ref[...]
        unit, scale = norm_parts(second + act_ref[...])
        sum_grad, gain_grad = norm_back(total[...], unit, scale, gain_ref[0:1, :])
        gain_out[...] = gain_grad
        both_pre_ref[0] = (sum_grad * (1.0 - second * second)).astype(BF16)
        spread[...] = sum_grad

    @pl.when(jnp.logical_and(step >= up_steps, step < up_steps + iso_steps))
    def _():
        sums = spread[...]
        for k in range(step_taps):
            back = taps - 1 - ((step - up_steps) * step_taps + k)
            grad = nt(both_pre_ref[0], iso_ref[k * width : (k + 1) * width, :])
            grad = jnp.where(since_ref[...] >= back, grad, 0.0)
            sums = sums + pltpu.roll(grad, blocks - back, 0)
        spread[...] = sums

    @pl.when(step == up_steps + iso_steps - 1)
    def _():
        active = act_ref[...]
        both_pre_ref[1] = (spread[...] * (1.0 - active * active)).astype(BF16)

    @pl.when(step >= up_steps + iso_steps)
    def _():
        for k in range(step_taps):
            block_ref[k] = nt(
                both_pre_ref[1], down_ref[k * width : (k + 1) * width, :]
            ).astype(BF16)


def scale_backward(pre, up, iso, down, act, second, since, gains):
    stride, blocks, width = pre.shape
    taps = iso.shape[0] // width
    step_taps = STEP_TAPS
    us, isteps = stride // step_taps, taps // step_taps
    whole = lambda shape: pl.BlockSpec(
        shape, lambda t: (0,) * len(shape), pipeline_mode=pl.Buffered(1)
    )
    clip = lambda value, top: jnp.minimum(jnp.maximum(value, 0), top)
    return pl.pallas_call(
        functools.partial(scale_backward_kernel, stride, taps, step_taps),
        grid=(2 * us + isteps,),
        in_specs=[
            pl.BlockSpec((step_taps, blocks, width), lambda t: (clip(t, us - 1), 0, 0)),
            pl.BlockSpec((width, step_taps * width), lambda t: (0, clip(t, us - 1))),
            pl.BlockSpec((step_taps * width, width), lambda t: (clip(t - us, isteps - 1), 0)),
            pl.BlockSpec(
                (step_taps * width, width), lambda t: (clip(t - us - isteps, us - 1), 0)
            ),
            whole(act.shape), whole(second.shape), whole(since.shape), whole(gains.shape),
        ],
        out_specs=[
            pl.BlockSpec((2, blocks, width), lambda t: (0, 0, 0)),
            pl.BlockSpec(
                (step_taps, blocks, width), lambda t: (clip(t - us - isteps, us - 1), 0, 0)
            ),
            pl.BlockSpec((1, width), lambda t: (0, 0)),
        ],
        out_shape=[
            jax.ShapeDtypeStruct((2, blocks, width), BF16),
            jax.ShapeDtypeStruct((stride, blocks, width), BF16),
            jax.ShapeDtypeStruct((1, width), F32),
        ],
        scratch_shapes=[pltpu.VMEM((blocks, width), F32), pltpu.VMEM((blocks, width), F32)],
        compiler_params=pltpu.CompilerParams(vmem_limit_bytes=VMEM_LIMIT),
        name="scale_backward",
    )(pre, up, iso, down, act, second, since, gains)


def split_spec(grid, in_specs, out_specs, scratch):
    return pltpu.PrefetchScalarGridSpec(
        num_scalar_prefetch=1, grid=grid, in_specs=in_specs, out_specs=out_specs,
        scratch_shapes=scratch,
    )


def up_grad_kernel(
    orders, mine_ref, own_joined, other_joined, own_pre, other_pre, *rest,
):
    *out_refs, turned = rest
    blocks = own_joined.shape[1]

    @pl.when(jnp.logical_and(pl.program_id(0) == 0, pl.program_id(1) == 0))
    def _():
        turned[:, :blocks] = flip(own_joined[0])
        turned[:, blocks:] = flip(other_joined[0])

    rows = jnp.concatenate([own_pre[0], other_pre[0]], axis=0)
    product = nn(turned[...], rows).astype(BF16)
    panels, height, _ = out_refs[0].shape[4:]
    for piece, (order, out_ref) in enumerate(zip(orders, out_refs)):
        for r in range(ROW_PARTS):
            for p in range(panels):
                low = (piece * panels + p) * LANES
                out_ref[(*part_at(order, r, 0), p)] = product[
                    r * height : (r + 1) * height, low : low + LANES
                ]


def up_grad(mine, joined, pre, orders):
    stride, blocks, width = pre[0].shape
    taps, panels = stride // COLUMN_PARTS, width // (LANES * len(orders))
    half = COLUMN_PARTS // 2
    height = width // ROW_PARTS

    def out_spec(order):
        sizes = tuple(1 if label == "x" else 2 for label in ORDERS[order])
        return pl.BlockSpec(
            (*sizes, panels, height, LANES),
            lambda x, j, mine: (
                *[x if label == "x" else 0 for label in ORDERS[order]], j, 0, 0
            ),
        )

    joined_spec = pl.BlockSpec((1, blocks, width), lambda x, j, mine: (0, 0, 0))
    pre_spec = pl.BlockSpec(
        (1, blocks, width), lambda x, j, mine: ((2 * x + mine[0]) * taps + j, 0, 0)
    )
    return pl.pallas_call(
        functools.partial(up_grad_kernel, orders),
        grid_spec=split_spec(
            (half, taps),
            [joined_spec, joined_spec, pre_spec, pre_spec],
            [out_spec(order) for order in orders],
            [pltpu.VMEM((width, 2 * blocks), BF16)],
        ),
        out_shape=[
            jax.ShapeDtypeStruct((2, 2, 2, 2, taps * panels, height, LANES), BF16)
            for _ in orders
        ],
        compiler_params=pltpu.CompilerParams(vmem_limit_bytes=VMEM_LIMIT),
        name="up_grad",
    )(mine, *joined, *pre)


def turn_half(turned, own_pre, other_pre, which, mine):
    blocks = own_pre.shape[1]
    for side, pre_ref in enumerate((own_pre, other_pre)):
        flipped = flip(pre_ref[which])
        there = slice(side * blocks, (side + 1) * blocks)
        for x in range(COLUMN_PARTS // 2):
            even = flipped[2 * x * LANES : (2 * x + 1) * LANES, :]
            odd = flipped[(2 * x + 1) * LANES : (2 * x + 2) * LANES, :]
            lines = slice(x * LANES, (x + 1) * LANES)

            @pl.when(mine == 0)
            def _(even=even, lines=lines, there=there):
                turned[lines, there] = even

            @pl.when(mine == 1)
            def _(odd=odd, lines=lines, there=there):
                turned[lines, there] = odd


def store_parts(orders, out_refs, k, product):
    per_part = out_refs[0].shape[4]
    panels = product.shape[1] // LANES
    for p in range(panels):
        r, at = divmod(panels * k + p, per_part * len(out_refs))
        piece, at = divmod(at, per_part)
        for x in range(COLUMN_PARTS // 2):
            out_refs[piece][(*part_at(orders[piece], r, x), at)] = product[
                x * LANES : (x + 1) * LANES, p * LANES : (p + 1) * LANES
            ]


GRAD_STEPS = 4


def grad_output(taps, width, order, pieces):
    per_part = taps * width // (ROW_PARTS * LANES * pieces)
    sizes = tuple(1 if label in ("near", "far") else 2 for label in ORDERS[order])
    spec = pl.BlockSpec(
        (*sizes, per_part, LANES, LANES),
        lambda t, mine: (
            *[{"near": t % 2, "far": t // 2}.get(label, 0) for label in ORDERS[order]], 0, 0, 0
        ),
    )
    return spec, jax.ShapeDtypeStruct((2, 2, 2, 2, per_part, LANES, LANES), BF16)


def grad_call(kernel, name, taps, width, blocks, orders, arguments, mine):
    whole = lambda shape: pl.BlockSpec(
        shape, lambda t, mine: (0,) * len(shape), pipeline_mode=pl.Buffered(1)
    )
    tapped = pl.BlockSpec((taps // GRAD_STEPS, blocks, width), lambda t, mine: (t, 0, 0))
    specs, shapes = zip(*[grad_output(taps, width, order, len(orders)) for order in orders])
    return pl.pallas_call(
        kernel,
        grid_spec=split_spec(
            (GRAD_STEPS,),
            [tapped if value.shape[0] == taps else whole(value.shape) for value in arguments],
            list(specs),
            [pltpu.VMEM((width // 2, 2 * blocks), BF16)],
        ),
        out_shape=list(shapes),
        compiler_params=pltpu.CompilerParams(vmem_limit_bytes=VMEM_LIMIT),
        name=name,
    )(mine, *arguments)


def iso_grad_kernel(
    taps, orders, mine_ref, own_pre, other_pre, own_act, other_act, own_since, other_since, *rest
):
    *out_refs, turned = rest
    step = pl.program_id(0)
    step_taps = taps // GRAD_STEPS

    @pl.when(step == 0)
    def _():
        turn_half(turned, own_pre, other_pre, 0, mine_ref[0])

    for k in range(step_taps):
        back = taps - 1 - (step * step_taps + k)
        rows = []
        for act_ref, since_ref in ((own_act, own_since), (other_act, other_since)):
            act = act_ref[1] if len(act_ref.shape) == 3 else act_ref[...]
            moved = pltpu.roll(act.astype(F32), back, 0)
            rows.append(jnp.where(since_ref[...] >= back, moved, 0.0).astype(BF16))
        rows = jnp.concatenate(rows, axis=0)
        store_parts(orders, out_refs, k, nn(turned[...], rows).astype(BF16))


def iso_grad(mine, pre, act, since, taps, orders):
    blocks, width = act[0].shape
    kernel = functools.partial(iso_grad_kernel, taps, orders)
    return grad_call(
        kernel, "iso_grad", taps, width, blocks, orders, (*pre, *act, *since), mine
    )


def down_grad_kernel(
    stride, orders, mine_ref, own_pre, other_pre, own_seasonal, other_seasonal, *rest
):
    *out_refs, turned = rest
    step_taps = stride // GRAD_STEPS

    @pl.when(pl.program_id(0) == 0)
    def _():
        turn_half(turned, own_pre, other_pre, 1, mine_ref[0])

    for k in range(step_taps):
        rows = jnp.concatenate([own_seasonal[k], other_seasonal[k]], axis=0)
        store_parts(orders, out_refs, k, nn(turned[...], rows).astype(BF16))


def down_grad(mine, pre, seasonal, orders):
    _, blocks, width = pre[0].shape
    stride = seasonal[0].shape[0]
    kernel = functools.partial(down_grad_kernel, stride, orders)
    return grad_call(
        kernel, "down_grad", stride, width, blocks, orders, (*pre, *seasonal), mine
    )


def back_kernel(
    sres_ref, block_a_ref, block_b_ref, cot_ref, head_ref, signal_ref, flags_ref, marks_ref,
    weight_ref, series_ref, embed_ref, season, low_near, low_wide, hidden,
):
    length, width = sres_ref.shape
    variates = signal_ref.shape[1]
    stride_a, per_a = block_a_ref.shape[0], block_a_ref.shape[1]
    stride_b, per_b = block_b_ref.shape[0], block_b_ref.shape[1]

    @pl.when(pl.program_id(0) == 0)
    def _():
        embed_ref[...] = jnp.zeros_like(embed_ref)

    placed(season, slice(0, length), sres_ref[...])
    for j in range(stride_a):
        at = pl.ds(j, per_a, stride=stride_a)
        placed(season, at, picked(season, at) + block_a_ref[j].astype(F32))
    for j in range(stride_b):
        at = pl.ds(j, per_b, stride=stride_b)
        placed(season, at, picked(season, at) + block_b_ref[j].astype(F32))
    result_grad = nt(cot_ref[...], head_ref[...]).astype(BF16).astype(F32)
    gap = result_grad - picked(season, slice(0, length))
    low_near[...] = (gap * flags_ref[:, 2:3]).astype(BF16)
    low_wide[...] = (gap * flags_ref[:, 3:4]).astype(BF16)
    for at, low, tile, span in tiles_of(length):
        near, wide = bands(
            flags_ref[at : at + tile, 4:5], marks_ref[0, :, low : low + span], at, low
        )
        total = picked(season, slice(at, at + tile)) + nn(near, low_near[low : low + span, :])
        total = total + nn(wide, low_wide[low : low + span, :])
        hidden[at : at + tile, :] = total.astype(BF16)
    grad = hidden[...]
    first = nt(grad, weight_ref[0:variates, :]) * flags_ref[:, 0:1]
    last = nt(grad, weight_ref[2 * variates :, :]) * flags_ref[:, 1:2]
    series_ref[...] = (
        nt(grad, weight_ref[variates : 2 * variates, :])
        + pltpu.roll(first, length - 1, 0)
        + pltpu.roll(last, 1, 0)
    )
    signal = signal_ref[...].astype(F32)
    before = (pltpu.roll(signal, 1, 0) * flags_ref[:, 0:1]).astype(BF16)
    after = (pltpu.roll(signal, length - 1, 0) * flags_ref[:, 1:2]).astype(BF16)
    embed_ref[0:variates, :] += tn(before, grad)
    embed_ref[variates : 2 * variates, :] += tn(signal_ref[...], grad)
    embed_ref[2 * variates :, :] += tn(after, grad)


def back(sres, block_a, block_b, cot, head, signal, flags, marks_row, weight, length):
    positions, width = sres.shape
    variates = signal.shape[1]
    stride_a, stride_b = block_a.shape[0], block_b.shape[0]
    whole = lambda shape: pl.BlockSpec(shape, lambda i: (0,) * len(shape))
    by_row = lambda size: pl.BlockSpec((length, size), lambda i: (i, 0))
    return pl.pallas_call(
        back_kernel,
        grid=(positions // length,),
        in_specs=[
            by_row(width),
            pl.BlockSpec((stride_a, length // stride_a, width), lambda i: (0, i, 0)),
            pl.BlockSpec((stride_b, length // stride_b, width), lambda i: (0, i, 0)),
            by_row(cot.shape[1]), whole(head.shape), by_row(variates), by_row(flags.shape[1]),
            pl.BlockSpec((1, 1, length), lambda i: (i, 0, 0)), whole(weight.shape),
        ],
        out_specs=[by_row(variates), whole(weight.shape)],
        out_shape=[
            jax.ShapeDtypeStruct((positions, variates), F32),
            jax.ShapeDtypeStruct(weight.shape, F32),
        ],
        scratch_shapes=[
            pltpu.VMEM((width // LANES, length, LANES), F32), pltpu.VMEM((length, width), BF16),
            pltpu.VMEM((length, width), BF16), pltpu.VMEM((length, width), BF16),
        ],
        compiler_params=pltpu.CompilerParams(vmem_limit_bytes=VMEM_LIMIT),
        name="back",
    )(sres, block_a, block_b, cot, head, signal, flags, marks_row, weight)


def block_diagonal(pieces):
    count, height, width = pieces.shape
    eye = jnp.eye(count, dtype=pieces.dtype)
    spread = pieces[:, :, None, :] * eye[:, None, :, None]
    return spread.reshape(count * height, count * width)


def diagonal_blocks(matrix, count):
    height, width = matrix.shape[0] // count, matrix.shape[1] // count
    blocks = matrix.reshape(count, height, count, width)
    kept = jnp.eye(count, dtype=jnp.bool_)[:, None, :, None]
    return jnp.sum(jnp.where(kept, blocks, 0.0), axis=2)


def same_window(marks, offset):
    length = marks.shape[1]
    filler = jnp.full_like(marks[:, : abs(offset)], -1)
    if offset > 0:
        moved = jnp.concatenate([filler, marks[:, : length - offset]], axis=1)
    else:
        moved = jnp.concatenate([marks[:, -offset:], filler], axis=1)
    return (moved == marks).astype(F32)


def window_flags(marks):
    near = jnp.ones(marks.shape, F32)
    for offset in range(1, 7):
        near = near + same_window(marks, offset) + same_window(marks, -offset)
    wide = near
    for offset in range(7, 9):
        wide = wide + same_window(marks, offset) + same_window(marks, -offset)
    zero = jnp.zeros_like(near)
    columns = [
        same_window(marks, 1), same_window(marks, -1), 0.5 / near, 0.5 / wide,
        marks.astype(F32), zero, zero, zero,
    ]
    return jnp.stack(columns, axis=-1).reshape(-1, len(columns))


def blocks_since_start(marks, stride, taps):
    coarse = marks[:, ::stride]
    since = jnp.zeros(coarse.shape, F32)
    for offset in range(1, taps):
        since = since + same_window(coarse, offset)
    return since.astype(jnp.int32).reshape(-1, 1)


BITS = {"core": ("var", 0), "x": ("var", 1), "y": ("rows", 0), "near": ("rows", 1), "far": ("rows", 2)}


def own_bit(label):
    axis, bit = BITS[label]
    return (lax.axis_index(axis) >> bit) & 1


def cross(values, label):
    axis, bit = BITS[label]
    flipped = (1 << bit, 0) if axis == "rows" else (0, 1 << bit)
    pairs = [
        (r * COLUMN_PARTS + c, (r ^ flipped[0]) * COLUMN_PARTS + (c ^ flipped[1]))
        for r in range(ROW_PARTS)
        for c in range(COLUMN_PARTS)
    ]
    return lax.ppermute(values, ("rows", "var"), pairs)


class Turns:
    def __init__(self):
        self.last = ()

    def seen(self, *values):
        self.last = values

    def after(self, small):
        return lax.optimization_barrier((small, *self.last))[0]


LINKS = ("x", "y", "near", "far")


class Place:
    def __init__(self, base=0, times=()):
        self.base, self.times = base, dict(times)

    def plus(self, base, label=None, times=0):
        moved = Place(self.base + base, self.times)
        if label is not None:
            moved.times[label] = moved.times.get(label, 0) + times
        return moved

    def value(self, bits_ref):
        line = jnp.int32(self.base)
        for label, times in self.times.items():
            line = line + bits_ref[LINKS.index(label)] * times
        return pl.multiple_of(line, LANES)


class Halving:
    def __init__(self, order):
        self.left = list(ORDERS[order])

    def start(self, *terms, lines=None):
        self.lines = lines or terms[0].size // (16 * LANES)
        self.terms = [term.reshape(-1, LANES) for term in terms]
        self.places = [Place() for _ in terms]


def fetch_terms(bits_ref, term_refs, terms, store, sems):
    copies, at = [], 0
    for n, (array, place, lines) in enumerate(terms):
        copy = pltpu.make_async_copy(
            term_refs[array].at[pl.ds(place.value(bits_ref), lines)],
            store.at[pl.ds(at, lines)], sems.at[n],
        )
        copy.start()
        copies.append((copy, at))
        at += lines
    return copies


def sum_lines(store, starts, line, count):
    total = store[pl.ds(starts[0] + line, count), :].astype(F32)
    for start in starts[1:]:
        total = total + store[pl.ds(start + line, count), :].astype(F32)
    return total


def send_kernel(plan, unique, bits_ref, *refs):
    term_refs = refs[:unique]
    out_refs, (store, sems) = refs[unique:-2], refs[-2:]
    terms = [term for _, _, _, group in plan for term in group]
    copies = fetch_terms(bits_ref, term_refs, terms, store, sems)
    for out, at, lines, group in plan:
        mine, copies = copies[: len(group)], copies[len(group) :]
        for copy, _ in mine:
            copy.wait()
        starts = [start for _, start in mine]
        out_ref = out_refs[out]

        def part(n, carry, at=at, starts=starts, out_ref=out_ref):
            line = pl.multiple_of(n * LANES, LANES)
            there = pl.ds(pl.multiple_of(at + line, LANES), LANES)
            out_ref[there, :] = sum_lines(store, starts, line, LANES).astype(BF16)
            return carry

        lax.fori_loop(0, lines // LANES, part, 0)


def unique_arrays(lists):
    arrays, where = [], []
    for values in lists:
        places = []
        for value in values:
            at = [n for n, one in enumerate(arrays) if one is value]
            if not at:
                at = [len(arrays)]
                arrays.append(value)
            places.append(at[0])
        where.append(places)
    return arrays, where


def call_with_terms(kernel, bits, arrays, lines, copies, out_shape, name):
    return pl.pallas_call(
        kernel,
        grid_spec=pltpu.PrefetchScalarGridSpec(
            num_scalar_prefetch=1, grid=(1,),
            in_specs=[pl.BlockSpec(memory_space=pl.ANY)] * len(arrays),
            out_specs=[
                pl.BlockSpec(one.shape, lambda t, bits: (0, 0), pipeline_mode=pl.Buffered(1))
                for one in out_shape
            ],
            scratch_shapes=[
                pltpu.VMEM((lines, LANES), BF16), pltpu.SemaphoreType.DMA((copies,)),
            ],
        ),
        out_shape=out_shape,
        compiler_params=pltpu.CompilerParams(vmem_limit_bytes=VMEM_LIMIT),
        name=name,
    )(bits, *arrays)


def step_together(turns, bits, chains):
    arrays, where = unique_arrays([one.terms for one in chains])
    by_label, plan, moves = {}, [], []
    for one, places in zip(chains, where):
        label = one.left.pop(0)
        lines = one.lines << len(one.left)
        out = list(by_label).index(label) if label in by_label else len(by_label)
        at = by_label.get(label, 0)
        by_label[label] = at + lines
        away = [place.plus(lines, label, -lines) for place in one.places]
        plan.append((out, at, lines, [(n, p, lines) for n, p in zip(places, away)]))
        moves.append((one, label, out, at, lines))
    terms = [term for entry in plan for term in entry[3]]
    sent = call_with_terms(
        functools.partial(send_kernel, plan, len(arrays)), turns.after(bits), arrays,
        sum(lines for _, _, lines in terms), len(terms),
        [jax.ShapeDtypeStruct((lines, LANES), BF16) for lines in by_label.values()], "send",
    )
    turns.seen(*sent)
    got = [cross(values, label) for values, label in zip(sent, by_label)]
    for one, label, out, at, lines in moves:
        one.places = [place.plus(0, label, lines) for place in one.places] + [Place(at)]
        one.terms.append(got[out])
    return got


def finish_kernel(plan, unique, bits_ref, *refs):
    term_refs = refs[:unique]
    out_refs, (store, sems) = refs[unique:-2], refs[-2:]
    terms = [term for group, _ in plan for term in group]
    copies = fetch_terms(bits_ref, term_refs, terms, store, sems)
    for group, pieces in plan:
        mine, copies = copies[: len(group)], copies[len(group) :]
        for copy, _ in mine:
            copy.wait()
        starts = [start for _, start in mine]
        line = 0
        for out, height, panels in pieces:
            for p in panels:
                block = sum_lines(store, starts, line, height)
                there = slice(p * LANES, (p + 1) * LANES)
                if height == LANES:
                    out_refs[out][there, :] = block.T
                else:
                    out_refs[out][:, there] = block
                line += height


def finish_together(bits, chains, shapes, pieces):
    arrays, where = unique_arrays([one.terms for one in chains])
    plan = []
    for one, places, mine in zip(chains, where, pieces):
        plan.append(([(n, p, one.lines) for n, p in zip(places, one.places)], mine))
    terms = [term for entry in plan for term in entry[0]]
    return call_with_terms(
        functools.partial(finish_kernel, plan, len(arrays)), bits, arrays,
        sum(lines for _, _, lines in terms), len(terms),
        [jax.ShapeDtypeStruct(shape, F32) for shape in shapes], "finish",
    )


def other_core(values):
    return lax.ppermute(
        values, "var", [(c, c ^ 1) for c in range(lax.axis_size("var"))]
    )


def both_halves(home, away, order, mine):
    home, away = from_part_order(home, order), from_part_order(away, order)
    first = jnp.where(mine == 0, home, away)
    second = jnp.where(mine == 0, away, home)
    halves = jnp.stack([first, second], axis=2)
    return halves.reshape(ROW_PARTS * COLUMN_PARTS, -1, LANES)


def scattered(full):
    rows, columns = lax.axis_size("rows"), lax.axis_size("var")
    height, depth = full.shape
    full = full.reshape(rows, height // rows, columns, depth // columns)
    full = full.transpose(0, 2, 1, 3).reshape(-1, depth // columns)
    return lax.psum_scatter(full, ("rows", "var"), scatter_dimension=0, tiled=True).astype(F32)


def scattered_columns(parts):
    width = COLUMN_PARTS * LANES
    panels = parts.reshape(ROW_PARTS, COLUMN_PARTS, -1, LANES, LANES)
    return scattered(panels.transpose(0, 2, 4, 1, 3).reshape(-1, width))


def scattered_features(parts, height):
    panels = parts.reshape(ROW_PARTS, COLUMN_PARTS, -1, height, LANES)
    return scattered(panels.transpose(0, 3, 1, 2, 4).reshape(ROW_PARTS * height, -1))


def sum_over(values, *labels):
    for label in labels:
        values = values + cross(values, label)
    return values


def body(
    signal_matrix, frame_numbers, variate_order, embed_weight, head_weight,
    down_a, iso_a, up_a, down_b, iso_b, up_b, merge_weight, ff_in, ff_out,
    norm_gains, estimate_cotangent,
):
    rows, columns = lax.axis_size("rows"), lax.axis_size("var")
    var_index = lax.axis_index("var")
    local_rows, length, variates = signal_matrix.shape
    local_groups = embed_weight.shape[0]
    per_group = head_weight.shape[2]
    groups = local_groups * columns
    time_rows = local_rows // columns
    width = norm_gains.shape[1]
    both_weights = jnp.concatenate([embed_weight, head_weight.transpose(0, 2, 1)], axis=1)
    both_weights = lax.all_gather(both_weights, "var", axis=0, tiled=True)
    taps = embed_weight.shape[1]
    embed_all, head_all = both_weights[:, :taps], both_weights[:, taps:].transpose(0, 2, 1)
    cotangent = lax.all_to_all(
        estimate_cotangent, "var", split_axis=0, concat_axis=2, tiled=True
    ).reshape(-1, variates)
    pick = jax.nn.one_hot(variate_order, variates, dtype=BF16)
    by_group = [
        block_diagonal(embed_all[:, tap * per_group : (tap + 1) * per_group]) for tap in range(3)
    ]
    by_signal = jnp.concatenate([tn(pick, part).astype(BF16) for part in by_group], axis=0)
    by_group = jnp.concatenate(by_group, axis=0)
    head_matrix = block_diagonal(head_all)
    signal = lax.dynamic_slice_in_dim(signal_matrix, var_index * time_rows, time_rows, 0)
    signal = signal.reshape(-1, variates)
    marks = lax.dynamic_slice_in_dim(frame_numbers, var_index * time_rows, time_rows, 0)
    marks = lax.optimization_barrier(marks)
    flags = window_flags(marks)
    marks_row = marks.astype(F32).reshape(time_rows, 1, length)
    since_a = blocks_since_start(marks, SA, iso_a.shape[0] // width)
    since_b = blocks_since_start(marks, SB, iso_b.shape[0] // width)

    trend, seasonal, taps_of_a, taps_of_b = front(signal, flags, marks_row, by_signal, length)
    lifted_a, act_a, second_a, joined_a = scale_forward(
        taps_of_a, down_a, iso_a, up_a, since_a, norm_gains, SA
    )
    lifted_b, act_b, second_b, joined_b = scale_forward(
        taps_of_b, down_b, iso_b, up_b, since_b, norm_gains, SB
    )
    mixing = rows == ROW_PARTS and columns == COLUMN_PARTS
    mine = own_bit("core").reshape(1)
    pair = lambda values: (values, other_core(values))
    pair_marks = lax.dynamic_slice_in_dim(
        frame_numbers, (var_index ^ 1) * time_rows, time_rows, 0
    )
    since_a = (since_a, blocks_since_start(pair_marks, SA, iso_a.shape[0] // width))
    since_b = (since_b, blocks_since_start(pair_marks, SB, iso_b.shape[0] // width))
    taps_pair_a, taps_pair_b = pair(taps_of_a), pair(taps_of_b)
    joined_pair_a, joined_pair_b = pair(joined_a), pair(joined_b)
    act_pair_a, act_pair_b = (act_a, joined_pair_a[1]), (act_b, joined_pair_b[1])
    predicted, pre_a, pre_b, sres, late_parts, head_full, gains_late = tail(
        lifted_a, lifted_b, seasonal, trend, cotangent, merge_weight, ff_in, ff_out,
        head_matrix, norm_gains, mine, length,
    )
    turns = Turns()
    bits = jnp.stack([own_bit(label) for label in LINKS]).astype(jnp.int32)
    orders = {
        "late": ("nxy",), "up_b": ("xny", "yxn"), "up_a": ("xyn", "yxn"),
        "iso_a": ("nyx", "ynx"), "down_a": ("yxn",), "iso_b": ("xyn",),
        "down_b": ("nyx", "xny"),
    }
    chains = {
        name: [Halving(order) for order in pieces] for name, pieces in orders.items()
    }
    done = {}

    def go(*names, through=False):
        if mixing:
            got = step_together(turns, bits, [one for name in names for one in chains[name]])
            if through:
                turns.seen(*turns.last, *got)

    def produced(name, *pieces):
        done[name] = pieces
        turns.seen(*pieces)
        for one, piece in zip(chains[name], pieces):
            one.start(piece)

    def turn():
        return turns.after(mine)

    taps_a, taps_b = iso_a.shape[0] // width, iso_b.shape[0] // width
    turns.seen(
        late_parts, taps_pair_a[1], taps_pair_b[1], joined_pair_a[1], joined_pair_b[1]
    )
    done["late"] = (late_parts,)
    late_lines = late_parts.shape[-2]
    if mixing:
        chains["late"][0].start(
            late_parts, cross(late_parts[1].reshape(-1, LANES), "core"), lines=late_lines
        )
    pre_pair_b, pre_pair_a = pair(pre_b), pair(pre_a)
    both_pre_a, block_a, gain_a = scale_backward(
        pre_a, up_a, iso_a, down_a, act_a, second_a, since_a[0], turns.after(norm_gains)
    )
    turns.seen(both_pre_a)
    both_pre_pair_a = pair(both_pre_a)
    go("late")
    produced("up_b", *up_grad(turn(), joined_pair_b, pre_pair_b, orders["up_b"]))
    go("up_b")
    produced("up_a", *up_grad(turn(), joined_pair_a, pre_pair_a, orders["up_a"]))
    go("up_a")
    both_pre_b, block_b, gain_b = scale_backward(
        pre_b, up_b, iso_b, down_b, act_b, second_b, since_b[0], turns.after(norm_gains)
    )
    turns.seen(both_pre_b)
    both_pre_pair_b = pair(both_pre_b)
    produced(
        "iso_a", *iso_grad(turn(), both_pre_pair_a, act_pair_a, since_a, taps_a, orders["iso_a"])
    )
    go("late", "up_b", "up_a", "iso_a")
    produced("down_a", *down_grad(turn(), both_pre_pair_a, taps_pair_a, orders["down_a"]))
    produced(
        "iso_b", *iso_grad(turn(), both_pre_pair_b, act_pair_b, since_b, taps_b, orders["iso_b"])
    )
    produced("down_b", *down_grad(turn(), both_pre_pair_b, taps_pair_b, orders["down_b"]))
    go("late", "up_b", "up_a", "iso_a", "down_a", "iso_b", "down_b")
    series_grad, embed_full = back(
        sres, block_a, block_b, cotangent, head_matrix, signal, flags, marks_row,
        turns.after(by_group), length
    )
    turns.seen(embed_full)
    gains_grad = jnp.concatenate([gains_late[0:1] + gain_a + gain_b, gains_late[1:]], axis=0)
    embed_full = jnp.einsum(
        "cv,tvd->tcd", pick.astype(F32), embed_full.reshape(3, variates, width),
        precision=lax.Precision.HIGHEST,
    )
    embed_grad = jnp.concatenate([diagonal_blocks(embed_full[tap], groups) for tap in range(3)], 1)
    head_grad = diagonal_blocks(head_full, groups)
    outward = jnp.stack([predicted, series_grad]).reshape(2, time_rows, length, variates)
    outward = lax.all_to_all(outward, "var", split_axis=3, concat_axis=1, tiled=True)
    small = (embed_grad, head_grad, gains_grad)
    if mixing:
        flat = jnp.concatenate([part.reshape(-1, LANES) for part in small])
        flat = sum_over(flat, "core", "x")
        turns.seen(flat)
        go("late", "up_b", "up_a", "iso_a", "down_a", "iso_b", "down_b", through=True)
        flat = sum_over(flat, "y", "near", "far")
        turns.seen(*turns.last, flat)
        pieces, at = [], 0
        for part in small:
            lines = part.size // LANES
            pieces.append(flat[at : at + lines].reshape(part.shape))
            at += lines
        embed_sum, head_sum, gains_sum = pieces
    else:
        embed_sum, head_sum, gains_sum = lax.psum(small, ("rows", "var"))
    embed_sum = lax.dynamic_slice_in_dim(embed_sum, var_index * local_groups, local_groups, 0)
    head_sum = lax.dynamic_slice_in_dim(head_sum, var_index * local_groups, local_groups, 0)

    height = width // ROW_PARTS
    merge_lines = merge_weight.size // (ROW_PARTS * COLUMN_PARTS * LANES)
    in_lines = ff_in.size // (ROW_PARTS * COLUMN_PARTS * LANES)
    if mixing:
        go("iso_a", "down_a", "iso_b", "down_b", through=True)
        go("down_a", "iso_b", "down_b")

        def turned(out, one, first=0):
            return out, LANES, range(first, first + one.lines // LANES)

        def kept(out, one, piece):
            half = width // LANES // 2
            count = one.lines // height
            return out, height, [2 * half * (p // half) + half * piece + p % half for p in range(count)]

        late, down_a_one, iso_b_one = [
            chains[name][0] for name in ("late", "down_a", "iso_b")
        ]
        first_a, second_a = chains["iso_a"]
        first_b, second_b = chains["down_b"]
        shard = lambda weight: (weight.shape[0] // rows, weight.shape[1] // columns)
        ups = finish_together(
            turns.after(bits), [*chains["up_a"], *chains["up_b"], late],
            [shard(weight) for weight in (up_a, up_b, merge_weight, ff_in, ff_out)],
            [
                *[[kept(0, one, n)] for n, one in enumerate(chains["up_a"])],
                *[[kept(1, one, n)] for n, one in enumerate(chains["up_b"])],
                [
                    (2, LANES, range(merge_lines // LANES)),
                    (3, height, range(in_lines // height)),
                    (4, LANES, range((late.lines - merge_lines - in_lines) // LANES)),
                ],
            ],
        )
        turns.seen(*ups)
        downs = finish_together(
            turns.after(bits), [down_a_one, first_a, second_a, iso_b_one, first_b, second_b],
            [shard(weight) for weight in (down_a, iso_a, iso_b, down_b)],
            [
                [turned(0, down_a_one)], [turned(1, first_a)],
                [turned(1, second_a, first_a.lines // LANES)], [turned(2, iso_b_one)],
                [turned(3, first_b)], [turned(3, second_b, first_b.lines // LANES)],
            ],
        )
        summed = (downs[0], downs[1], ups[0], downs[3], downs[2], ups[1], *ups[2:])
    else:
        total = {}
        for name, pieces in done.items():
            if name == "late":
                halves = [(pieces[0][0], pieces[0][1])]
            else:
                halves = [(piece, jnp.zeros_like(piece)) for piece in pieces]
            parts = [
                both_halves(*two, order, mine[0]) for two, order in zip(halves, orders[name])
            ]
            if name.startswith("up"):
                half = width * height // (2 * LANES)
                parts = [part.reshape(part.shape[0], -1, half, LANES) for part in parts]
                total[name] = jnp.concatenate(parts, axis=2)
            else:
                total[name] = jnp.concatenate(parts, axis=1)
        turned, kept = scattered_columns, scattered_features
        split = (merge_lines, merge_lines + in_lines)
        merge_part, in_part, out_part = jnp.split(total["late"], split, axis=1)
        summed = (
            turned(total["down_a"]), turned(total["iso_a"]), kept(total["up_a"], height),
            turned(total["down_b"]), turned(total["iso_b"]), kept(total["up_b"], height),
            turned(merge_part), kept(in_part, height), turned(out_part),
        )
    return (outward[0], outward[1], embed_sum, head_sum, *summed, gains_sum)


def solution(mesh):
    placed = (
        P("rows", None, None),
        P("rows", None),
        P(),
        P("var", None, None),
        P("var", None, None),
        P(),
        P(),
        P(),
        P(),
        P(),
        P(),
        P(),
        P(),
        P(),
        P(),
        P("rows", None, "var"),
    )
    return jax.shard_map(
        body,
        mesh=mesh,
        in_specs=placed,
        out_specs=(
            P("rows", None, "var"),
            P("rows", None, "var"),
            P("var", None, None),
            P("var", None, None),
            P("rows", "var"),
            P("rows", "var"),
            P("rows", "var"),
            P("rows", "var"),
            P("rows", "var"),
            P("rows", "var"),
            P("rows", "var"),
            P("rows", "var"),
            P("rows", "var"),
            P(),
        ),
        check_vma=False,
    )
```
